128 devices in a mesh: leaf: 8 (over y, core), tile: 16 (over z, x).
Axes of the slice: x: 4, y: 4, z: 4, core: 2. Of those that a mesh axis runs over, the one named last changes fastest.
Arguments:
- right_sides: float32 [4, 4096, 128], P(None, ('leaf', 'tile')), may hold values from -6 to 6
- diag_inverse: bfloat16 [4096, 7680], P(('leaf', 'tile')), may hold values from -2.8 to 2.8, as said below
- coupling: bfloat16 [4096, 1088], P(('leaf', 'tile')), may hold values from -0.375 to 0.375
- pattern: int32 [128, 34], P(('leaf', 'tile')), may hold values 0 or 1
Outputs:
- solution: float32 [4, 4096, 128], P(None, ('leaf', 'tile'))
The draws below stay inside these ranges and needn't reach their ends.
Inputs may be any that keep to these rules, and one draw needn't show every extreme that they name: Within each supernode the block of diag_inverse is the inverse of a lower triangular diagonal block of the factor: zero above its diagonal and between 0.6 and 1.4 on it.
All inputs are finite; a program needn't handle non-finite values. No bound on the sum of `pattern` on one device may be relied on, other than what follows from the above.
Results may differ from the reference program's by a relative error of at most 0.018.
Values may be sent and summed in bfloat16 or wider, within the bound.
No kernel may reach another device: no remote copies, remote signals or barrier semaphores. Data moves between devices by JAX's collectives and lax.ppermute only.
A program may use at most 64 MiB of HBM per device.

```python
import jax
import jax.numpy as jnp
from jax import lax

R = 32
NRHS = 128
LEVELS = 4
PANEL = 512
ROWS = 4096
DCOLS = 7680
OFFB = 34
N_LEAF = 8
N_TILE = 16
DEVICES = 128


def draw_diag_inverse(key, part):
    values = jnp.clip(jax.random.normal(key, (ROWS, DCOLS), jnp.float32), -4.0, 4.0)
    row_ids = jnp.arange(ROWS, dtype=jnp.int32)[:, None]
    col_ids = jnp.arange(DCOLS, dtype=jnp.int32)[None, :]
    column_block = col_ids // PANEL
    tier_index = jnp.zeros_like(column_block)
    for height in range(1, LEVELS):
        tier_index = tier_index + (column_block >= 2 ** height - 1).astype(jnp.int32)
    group_span = jnp.left_shift(jnp.ones_like(tier_index), tier_index)
    within = col_ids - (group_span - 1) * PANEL
    position = row_ids % (group_span * PANEL)
    lower_mask = within < position
    diagonal = within == position
    scaled = 0.7 * values / jnp.sqrt(position.astype(jnp.float32) + 1.0)
    result = jnp.where(diagonal, 1.0 + 0.1 * values, jnp.where(lower_mask, scaled, 0.0))
    return result.astype(jnp.bfloat16)


def set_ends(values, own_key, smallest, high):
    index_at = [jax.random.randint(jax.random.fold_in(own_key, axis), (), 0, length) for axis, length in enumerate(values.shape)]
    main_axis = values.shape.index(max(values.shape))
    neighbour = index_at[:main_axis] + [(index_at[main_axis] + 1) % values.shape[main_axis]] + index_at[main_axis + 1:]
    return values.at[tuple(index_at)].set(smallest).at[tuple(neighbour)].set(high)


def levels(own_key, extent, split, least, high):
    factor_of, own = 1.0, jax.random.fold_in(own_key, 6)
    for axis_at, shards_of in split:
        heights = jnp.exp(jax.random.uniform(jax.random.fold_in(own, axis_at), (shards_of,), jnp.float32, least / len(split), high / len(split)))
        factor_of = factor_of * jnp.repeat(heights, extent[axis_at] // shards_of).reshape([-1 if axis == axis_at else 1 for axis in range(len(extent))])
    return factor_of


def normal_values(rng, dims, width, bound, pieces=(), held_as=jnp.bfloat16):
    loudness = levels(rng, dims, pieces, -0.22, 0.18) if pieces else 1.0
    drawn = jax.random.normal(rng, dims, jnp.float32) * width * loudness
    return jnp.minimum(jnp.maximum(drawn, -bound), bound).astype(held_as)


def setup_inputs(seed: int = 0) -> dict:
    streams_of = jax.random.split(jax.random.key(seed), 5)
    right_sides = normal_values(streams_of[0], (LEVELS, ROWS, NRHS), 1.0, 6.0, ((1, 128),), jnp.float32)
    diag_inverse = draw_diag_inverse(jax.random.fold_in(streams_of[4], 71), 0)
    coupling = normal_values(streams_of[2], (ROWS, OFFB * R), (R * OFFB // 4) ** -0.5, 0.375, ((0, 128),))
    pattern = set_ends((jax.random.randint(streams_of[3], (DEVICES, OFFB), 0, 2) < 1).astype(jnp.int32), jax.random.fold_in(streams_of[3], 1), 0, 1)
    return {"right_sides": right_sides, "diag_inverse": diag_inverse, "coupling": coupling, "pattern": pattern}


def pair_offsets():
    offset_map = {}
    cursor = 0
    for top_level in range(1, LEVELS):
        for low_level in range(top_level):
            offset_map[(top_level, low_level)] = cursor
            cursor += 2 ** top_level
    return offset_map


def coupling_part(masked, offset_map, top_level, low_level):
    group_span = 2 ** top_level
    first_col = offset_map[(top_level, low_level)] * R
    sub_part = masked[:, :, :, first_col:first_col + group_span * R]
    return sub_part.reshape(N_LEAF // group_span, group_span, N_TILE, R, group_span, R).astype(jnp.float32)


def apply_inverse(diag_inverse, vectors, height, transpose):
    group_span = 2 ** height
    node_order = group_span * PANEL
    matrices = diag_inverse[:, (group_span - 1) * PANEL:(2 * group_span - 1) * PANEL]
    matrices = matrices.reshape(N_LEAF // group_span, node_order, node_order)
    stacked = vectors.reshape(N_LEAF // group_span, node_order, NRHS)

    def one_node(operands):
        if transpose:
            return jnp.dot(operands[0].T, operands[1], preferred_element_type=jnp.float32)
        return jnp.dot(operands[0], operands[1], preferred_element_type=jnp.float32)

    return lax.map(one_node, (matrices, stacked)).reshape(ROWS, NRHS)


def reference(right_sides, diag_inverse, coupling, pattern):
    offset_map = pair_offsets()
    masked = coupling.reshape(DEVICES, R, OFFB, R) * pattern.astype(coupling.dtype)[:, None, :, None]
    masked = masked.reshape(N_LEAF, N_TILE, R, OFFB * R)
    solved = []
    for height in range(LEVELS):
        group_span = 2 ** height
        reduced = right_sides[height]
        for low_level in range(height):
            weights = coupling_part(masked, offset_map, height, low_level)
            source = solved[low_level].astype(jnp.float32).reshape(N_LEAF // group_span, group_span, N_TILE, R, NRHS)
            reduced = reduced - jnp.einsum("gatrkb,gktbn->gatrn", weights, source).reshape(ROWS, NRHS)
        forward = apply_inverse(diag_inverse, reduced.astype(jnp.bfloat16), height, False)
        solved.append(lax.optimization_barrier(forward.astype(jnp.bfloat16)))
    pending = [jnp.zeros((ROWS, NRHS), jnp.float32) for height in range(LEVELS)]
    answers = [None] * LEVELS
    for height in reversed(range(LEVELS)):
        group_span = 2 ** height
        remainder = (solved[height].astype(jnp.float32) - pending[height]).astype(jnp.bfloat16)
        answers[height] = apply_inverse(diag_inverse, remainder, height, True)
        answer_half = lax.optimization_barrier(answers[height].astype(jnp.bfloat16)).astype(jnp.float32)
        answer_half = answer_half.reshape(N_LEAF // group_span, group_span, N_TILE, R, NRHS)
        for low_level in range(height):
            weights = coupling_part(masked, offset_map, height, low_level)
            update = jnp.einsum("gatrkb,gatrn->gktbn", weights, answer_half).reshape(ROWS, NRHS)
            pending[low_level] = pending[low_level] + update
    return jnp.stack(answers, 0)
```

```python
import functools

import jax
import jax.numpy as jnp
from jax import lax
from jax.experimental import pallas as pl
from jax.experimental.pallas import tpu as pltpu
from jax.sharding import PartitionSpec as P

BF = jnp.bfloat16
F32 = jnp.float32
PAIRS = ((1, 0), (2, 0), (2, 1), (3, 0), (3, 1), (3, 2))
OFFSET = {(1, 0): 0, (2, 0): 2, (2, 1): 6, (3, 0): 10, (3, 1): 18, (3, 2): 26}
BLOCKS = 34
VMEM = pl.BlockSpec(memory_space=pltpu.VMEM)
SMEM = pl.BlockSpec(memory_space=pltpu.SMEM)
RHS_ROWS, C_TILES, D0_TILES, D1_TILES = 16, 9, 4, 8
C_AT = RHS_ROWS
D0_AT = C_AT + 32 * C_TILES
D1_AT = D0_AT + 32 * D0_TILES
MESSAGE = D1_AT + 32 * D1_TILES


def params(mib=48):
    return pltpu.CompilerParams(vmem_limit_bytes=mib * 2**20)


def lane_chunk(rows):
    return lax.broadcasted_iota(jnp.int32, (rows, 128), 1) // 32


def dot_nt(a, b):
    return lax.dot_general(a, b, (((1,), (1,)), ((), ())), preferred_element_type=F32)


def dot_nn(a, b):
    return jnp.dot(a, b, preferred_element_type=F32)


class Rolled:
    def __init__(self, tiles):
        self.tiles = tiles
        self.made = {}

    def take(self, tile, source, target):
        shift = (target - source) % 4 * 32
        if shift == 0:
            return self.tiles[tile]
        if (tile, shift) not in self.made:
            self.made[tile, shift] = pltpu.roll(self.tiles[tile], shift, 1)
        return self.made[tile, shift]


def merge(parts, chunk):
    result = parts[0]
    for c in range(1, len(parts)):
        result = jnp.where(chunk == c, parts[c], result)
    return result


def split_kernel(coupling_ref, pattern_ref, out_ref):
    chunk = lane_chunk(32)
    tiles = []
    for tile in range(C_TILES):
        if tile < 8:
            values = coupling_ref[:, 128 * tile : 128 * tile + 128].astype(F32)
        else:
            half = coupling_ref[:, 1024:1088].astype(F32)
            values = jnp.concatenate([half, jnp.zeros_like(half)], 1)
        keep = jnp.zeros((32, 128), F32)
        for c in range(4):
            if 4 * tile + c < BLOCKS:
                keep = jnp.where(chunk == c, pattern_ref[0, 4 * tile + c].astype(F32), keep)
        tiles.append(values * keep)
    rolled = Rolled(tiles)
    for leaf in range(8):
        parts = []
        for q, (w, u) in enumerate(PAIRS):
            block = OFFSET[w, u] + leaf % 2**w
            parts.append(rolled.take(block // 4, block % 4, q % 4))
        out_ref[leaf, :, 0:128] = merge(parts[:4], chunk).astype(BF)
        out_ref[leaf, :, 128:256] = merge(parts[4:], chunk).astype(BF)


def message_kernel(leaf_ref, columns_ref, rhs_ref, diag_ref, out_ref):
    leaf = leaf_ref[0]
    chunk = lane_chunk(32)
    common = []
    sources = []
    for w, u in PAIRS:
        q = PAIRS.index((w, u))
        for i in range(2**w):
            sources.append((leaf // 2**w * 2**w + i, q))
    for tile in range(C_TILES):
        parts = []
        for c in range(4):
            if 4 * tile + c < BLOCKS:
                source, q = sources[4 * tile + c]
                values = columns_ref[source, :, 128 * (q // 4) : 128 * (q // 4) + 128].astype(F32)
                shift = (c - q) % 4 * 32
                parts.append(values if shift == 0 else pltpu.roll(values, shift, 1))
        common.append(merge(parts, chunk).astype(BF))
    for tile in range(D0_TILES + D1_TILES):
        common.append(diag_ref[:, 128 * tile : 128 * tile + 128])
    rhs = jnp.transpose(rhs_ref[...].reshape(128, 128))
    high = rhs.astype(BF).astype(F32)
    low = rhs - high
    for tile in range(16):
        both = jnp.concatenate([high[8 * tile : 8 * tile + 8], low[8 * tile : 8 * tile + 8]], 0)
        out_ref[tile, 0:RHS_ROWS] = both.astype(BF)
        for n, values in enumerate(common):
            out_ref[tile, C_AT + 32 * n : C_AT + 32 * n + 32] = values


def couple(parts, bd_ref):
    out = []
    for j in range(4):
        total = None
        for vector, m in parts:
            term = dot_nt(vector[:, 128 * j : 128 * j + 128], bd_ref[m, j])
            total = term if total is None else total + term
        out.append(-total)
    return jnp.concatenate(out, 1)


def first_kernel(leaf_ref, msg_ref, b_ref, bd_ref, d0_ref, d1_ref, y0_ref, p1_ref):
    leaf = leaf_ref[0]
    chunk8 = lane_chunk(8)
    rhs = Rolled(
        [msg_ref[t, 0:8].astype(F32) + msg_ref[t, 8:16].astype(F32) for t in range(16)]
    )
    for v in range(4):
        for j in range(4):
            parts = [rhs.take(4 * j + c, v, c) for c in range(4)]
            b_ref[v, :, 128 * j : 128 * j + 128] = merge(parts, chunk8)
    row_chunk = lax.broadcasted_iota(jnp.int32, (128, 128), 0) // 32
    same = row_chunk == lane_chunk(128)
    rows = lax.broadcasted_iota(jnp.int32, (128, 128), 0)
    lanes = lax.broadcasted_iota(jnp.int32, (128, 128), 1)
    pick = [
        jnp.where(rows == lanes % 32 + 32 * c, 1.0, 0.0).astype(BF) for c in range(4)
    ]
    for m in range(BLOCKS):
        at = C_AT + 32 * (m // 4)
        for j in range(4):
            block = msg_ref[4 * j : 4 * j + 4, at : at + 32, :].reshape(128, 128)
            spread = dot_nn(block, pick[m % 4])
            bd_ref[m, j] = jnp.where(same, spread, 0.0).astype(BF)
    for tile in range(D0_TILES):
        at = D0_AT + 32 * tile
        d0_ref[:, 128 * tile : 128 * tile + 128] = msg_ref[:, at : at + 32, :].reshape(512, 128)
    for tile in range(D1_TILES):
        at = D1_AT + 32 * tile
        d1_ref[:, 128 * tile : 128 * tile + 128] = msg_ref[:, at : at + 32, :].reshape(512, 128)
    y0 = dot_nt(b_ref[0].astype(BF), d0_ref[...]).astype(BF)
    y0_ref[...] = y0
    for i in range(2):
        mine = jnp.where(leaf % 2 == i, b_ref[1], 0.0)
        p1_ref[:, 512 * i : 512 * i + 512] = (couple([(y0, i)], bd_ref) + mine).astype(BF)


def times_rows(z, d_ref, width):
    total = jnp.zeros((8, 512), F32)
    for at in range(0, width, 1024):
        total = total + dot_nt(z[:, at : at + 1024], d_ref[:, at : at + 1024])
    return total


def forward_kernel(level, leaf_ref, own_ref, other_ref, d_ref, b_ref, bd_ref, *rest):
    ys, (y_ref, p_ref) = rest[:-2], rest[-2:]
    leaf = leaf_ref[0]
    z = (own_ref[...].astype(F32) + other_ref[...].astype(F32)).astype(BF)
    y = times_rows(z, d_ref, z.shape[1]).astype(BF)
    y_ref[...] = y
    vectors = [r[...] for r in ys] + [y]
    span = 2 ** (level + 1)
    for i in range(span):
        mine = jnp.where(leaf % span == i, b_ref[level + 1], 0.0)
        parts = [(vec, OFFSET[level + 1, u] + i) for u, vec in enumerate(vectors)]
        p_ref[:, 512 * i : 512 * i + 512] = (couple(parts, bd_ref) + mine).astype(BF)


def top_kernel(own_ref, other_ref, d_ref, x_ref):
    z = (own_ref[...].astype(F32) + other_ref[...].astype(F32)).astype(BF)
    y = times_rows(z, d_ref, 4096).astype(BF)
    for at in range(0, 4096, 1024):
        x_ref[:, at : at + 1024] = dot_nn(y, d_ref[:, at : at + 1024]).astype(BF)


def back_kernel(level, leaf_ref, own_ref, other_ref, d_ref, y_ref, bd_ref, *rest):
    first = level == 2
    pending = () if first else rest[: level + 1]
    outs = rest[len(pending) :]
    x_ref, xp_ref, next_refs = outs[0], outs[1], outs[2:]
    leaf = leaf_ref[0]
    span = 2 ** (level + 1)
    total = own_ref[...].astype(F32) + other_ref[...].astype(F32)
    x = total.astype(BF)
    mine = total[:, 0:512]
    for i in range(1, span):
        mine = jnp.where(leaf % span == i, total[:, 512 * i : 512 * i + 512], mine)
    x_ref[...] = mine
    for u in range(level + 1):
        columns = []
        for j in range(4):
            term = None
            for i in range(span):
                at = 512 * i + 128 * j
                part = dot_nn(x[:, at : at + 128], bd_ref[OFFSET[level + 1, u] + i, j])
                term = part if term is None else term + part
            columns.append(term)
        p = jnp.concatenate(columns, 1)
        if not first:
            p = p + pending[u][...]
        if u < level:
            next_refs[u][...] = p
        else:
            q = (y_ref[...].astype(F32) - p).astype(BF)
    if level > 0:
        width = 512 * 2**level
        for at in range(0, width, 1024):
            xp_ref[:, at : at + 1024] = dot_nn(q, d_ref[:, at : at + 1024]).astype(BF)
    else:
        xp_ref[...] = dot_nn(q, d_ref[...])


def pack_kernel(x0_ref, x1_ref, x2_ref, x3_ref, out_ref):
    chunk = lane_chunk(8)
    tiles = [r[:, 128 * j : 128 * j + 128] for r in (x0_ref, x1_ref, x2_ref, x3_ref) for j in range(4)]
    rolled = Rolled(tiles)
    for t in range(16):
        parts = [rolled.take(4 * v + t // 4, t % 4, v) for v in range(4)]
        out_ref[t] = merge(parts, chunk)


def shape(dims, kind=BF):
    return jax.ShapeDtypeStruct(dims, kind)


def reduce_over(part, level):
    hops = [
        [(i, i ^ 1) for i in range(8)],
        [(i, i ^ 2) for i in range(8)],
        [(i, (3 - i // 2) * 2 + i % 2) for i in range(8)],
    ]
    for n in range(level):
        other = lax.ppermute(part, "leaf", hops[n])
        if n == level - 1:
            return part, other
        part = (part.astype(F32) + other.astype(F32)).astype(BF)


def local(right_sides, diag_inverse, coupling, pattern):
    leaf = lax.axis_index("leaf").astype(jnp.int32).reshape(1)
    d23 = lax.all_gather(diag_inverse[:, 1536:], "tile", axis=0, tiled=True)
    split = pl.pallas_call(
        split_kernel,
        out_shape=shape((8, 32, 256)),
        in_specs=[VMEM, SMEM],
        out_specs=VMEM,
        compiler_params=params(),
        name="split_couplings",
    )(coupling, pattern)
    columns = lax.all_to_all(split, "leaf", 0, 0, tiled=True)
    message = pl.pallas_call(
        message_kernel,
        out_shape=shape((16, MESSAGE, 128)),
        grid=(1,),
        in_specs=[
            SMEM,
            pl.BlockSpec((8, 32, 256), lambda i: (0, 0, 0)),
            pl.BlockSpec((4, 32, 128), lambda i: (0, 0, 0)),
            pl.BlockSpec((32, 1536), lambda i: (0, 0)),
        ],
        out_specs=pl.BlockSpec((16, MESSAGE, 128), lambda i: (0, 0, 0)),
        compiler_params=params(),
        name="message",
    )(leaf, columns, right_sides, diag_inverse)
    message = lax.all_to_all(message, "tile", 0, 0, tiled=True)
    b, bd, d0, d1, y0, p1 = pl.pallas_call(
        first_kernel,
        out_shape=(
            shape((4, 8, 512), F32),
            shape((BLOCKS, 4, 128, 128)),
            shape((512, 512)),
            shape((512, 1024)),
            shape((8, 512)),
            shape((8, 1024)),
        ),
        in_specs=[SMEM, VMEM],
        out_specs=(VMEM,) * 6,
        compiler_params=params(),
        name="level0",
    )(leaf, message)
    d2, d3 = d23[:, :2048], d23[:, 2048:]

    def forward(level, part, d, ys):
        own, other = reduce_over(part, level)
        return pl.pallas_call(
            functools.partial(forward_kernel, level),
            out_shape=(shape((8, 512)), shape((8, 512 * 2 ** (level + 1)))),
            in_specs=[SMEM] + [VMEM] * (5 + len(ys)),
            out_specs=(VMEM,) * 2,
            compiler_params=params(),
            name="forward%d" % level,
        )(leaf, own, other, d, b, bd, *ys)

    y1, p2 = forward(1, p1, d1, (y0,))
    y2, p3 = forward(2, p2, d2, (y0, y1))
    own, other = reduce_over(p3, 3)
    xp = pl.pallas_call(
        top_kernel,
        out_shape=shape((8, 4096)),
        in_specs=[VMEM] * 3,
        out_specs=VMEM,
        compiler_params=params(),
        name="level3",
    )(own, other, d3)

    def back(level, part, d, y, pending):
        own, other = reduce_over(part, level + 1)
        out = [shape((8, 512), F32)]
        out.append(shape((8, 512 * 2**level), BF if level else F32))
        out += [shape((8, 512), F32)] * level
        return pl.pallas_call(
            functools.partial(back_kernel, level),
            out_shape=tuple(out),
            in_specs=[SMEM] + [VMEM] * (5 + len(pending)),
            out_specs=(VMEM,) * len(out),
            compiler_params=params(),
            name="back%d" % level,
        )(leaf, own, other, d, y, bd, *pending)

    x3, xp, *pending = back(2, xp, d2, y2, ())
    x2, xp, *pending = back(1, xp, d1, y1, pending)
    x1, x0 = back(0, xp, d0, y0, pending)
    packed = pl.pallas_call(
        pack_kernel,
        out_shape=shape((16, 8, 128), F32),
        in_specs=[VMEM] * 4,
        out_specs=VMEM,
        compiler_params=params(),
        name="pack",
    )(x0, x1, x2, x3)
    packed = lax.all_to_all(packed, "tile", 0, 0, tiled=True)
    return jnp.transpose(packed.reshape(128, 128)).reshape(4, 32, 128)


def solution(mesh):
    placed = (
        P(None, ("leaf", "tile"), None),
        P(("leaf", "tile"), None),
        P(("leaf", "tile"), None),
        P(("leaf", "tile"), None),
    )
    return jax.shard_map(
        local,
        mesh=mesh,
        in_specs=placed,
        out_specs=P(None, ("leaf", "tile"), None),
        check_vma=False,
    )
```

```python
import functools

import jax
import jax.numpy as jnp
from jax import lax
from jax.experimental import pallas as pl
from jax.experimental.pallas import tpu as pltpu
from jax.sharding import PartitionSpec as P


BF = jnp.bfloat16
F32 = jnp.float32
PAIRS = ((1, 0), (2, 0), (2, 1), (3, 0), (3, 1), (3, 2))
OFFSET = {(1, 0): 0, (2, 0): 2, (2, 1): 6, (3, 0): 10, (3, 1): 18, (3, 2): 26}
BLOCKS = 34
VMEM = pl.BlockSpec(memory_space=pltpu.VMEM)
SMEM = pl.BlockSpec(memory_space=pltpu.SMEM)
RHS_ROWS, C_TILES, D0_TILES, D1_TILES, D2_TILES = 16, 9, 4, 8, 16
C_AT = RHS_ROWS
D0_AT = C_AT + 32 * C_TILES
D1_AT = D0_AT + 32 * D0_TILES
D2_AT = D1_AT + 32 * D1_TILES
MESSAGE = D2_AT + 32 * D2_TILES


def params(mib=48):
    return pltpu.CompilerParams(vmem_limit_bytes=mib * 2**20)


def lane_chunk(rows):
    return lax.broadcasted_iota(jnp.int32, (rows, 128), 1) // 32


def dot_nt(a, b):
    return lax.dot_general(a, b, (((1,), (1,)), ((), ())), preferred_element_type=F32)


def dot_nn(a, b):
    return jnp.dot(a, b, preferred_element_type=F32)


class Rolled:
    def __init__(self, tiles):
        self.tiles = tiles
        self.made = {}

    def take(self, tile, source, target):
        shift = (target - source) % 4 * 32
        if shift == 0:
            return self.tiles[tile]
        if (tile, shift) not in self.made:
            self.made[tile, shift] = pltpu.roll(self.tiles[tile], shift, 1)
        return self.made[tile, shift]


def merge(parts, chunk):
    result = parts[0]
    for c in range(1, len(parts)):
        result = jnp.where(chunk == c, parts[c], result)
    return result


def split_kernel(coupling_ref, pattern_ref, out_ref):
    chunk = lane_chunk(32)
    tiles = []
    for tile in range(C_TILES):
        if tile < 8:
            values = coupling_ref[:, 128 * tile : 128 * tile + 128].astype(F32)
        else:
            half = coupling_ref[:, 1024:1088].astype(F32)
            values = jnp.concatenate([half, jnp.zeros_like(half)], 1)
        keep = jnp.zeros((32, 128), F32)
        for c in range(4):
            if 4 * tile + c < BLOCKS:
                keep = jnp.where(chunk == c, pattern_ref[0, 4 * tile + c].astype(F32), keep)
        tiles.append(values * keep)
    rolled = Rolled(tiles)
    for leaf in range(8):
        parts = []
        for q, (w, u) in enumerate(PAIRS):
            block = OFFSET[w, u] + leaf % 2**w
            parts.append(rolled.take(block // 4, block % 4, q % 4))
        out_ref[leaf, :, 0:128] = merge(parts[:4], chunk).astype(BF)
        out_ref[leaf, :, 128:256] = merge(parts[4:], chunk).astype(BF)


def message_kernel(leaf_ref, columns_ref, rhs_ref, diag_ref, out_ref):
    leaf = leaf_ref[0]
    chunk = lane_chunk(32)
    common = []
    sources = []
    for w, u in PAIRS:
        q = PAIRS.index((w, u))
        for i in range(2**w):
            sources.append((leaf // 2**w * 2**w + i, q))
    for tile in range(C_TILES):
        parts = []
        for c in range(4):
            if 4 * tile + c < BLOCKS:
                source, q = sources[4 * tile + c]
                values = columns_ref[source, :, 128 * (q // 4) : 128 * (q // 4) + 128].astype(F32)
                shift = (c - q) % 4 * 32
                parts.append(values if shift == 0 else pltpu.roll(values, shift, 1))
        common.append(merge(parts, chunk).astype(BF))
    for tile in range(D0_TILES + D1_TILES + D2_TILES):
        common.append(diag_ref[:, 128 * tile : 128 * tile + 128])
    rhs = jnp.transpose(rhs_ref[...].reshape(128, 128))
    high = rhs.astype(BF).astype(F32)
    low = rhs - high
    for tile in range(16):
        both = jnp.concatenate([high[8 * tile : 8 * tile + 8], low[8 * tile : 8 * tile + 8]], 0)
        out_ref[tile, 0:RHS_ROWS] = both.astype(BF)
        for n, values in enumerate(common):
            out_ref[tile, C_AT + 32 * n : C_AT + 32 * n + 32] = values


def couple(parts, bd_ref):
    out = []
    for j in range(4):
        total = None
        for vector, m in parts:
            term = dot_nt(vector[:, 128 * j : 128 * j + 128], bd_ref[m, j])
            total = term if total is None else total + term
        out.append(-total)
    return jnp.concatenate(out, 1)


def first_kernel(leaf_ref, msg_ref, b_ref, bd_ref, d0_ref, d1_ref, d2_ref, y0_ref, p1_ref):
    leaf = leaf_ref[0]
    chunk8 = lane_chunk(8)
    rhs = Rolled(
        [msg_ref[t, 0:8].astype(F32) + msg_ref[t, 8:16].astype(F32) for t in range(16)]
    )
    for v in range(4):
        for j in range(4):
            parts = [rhs.take(4 * j + c, v, c) for c in range(4)]
            b_ref[v, :, 128 * j : 128 * j + 128] = merge(parts, chunk8)
    row_chunk = lax.broadcasted_iota(jnp.int32, (128, 128), 0) // 32
    same = row_chunk == lane_chunk(128)
    rows = lax.broadcasted_iota(jnp.int32, (128, 128), 0)
    lanes = lax.broadcasted_iota(jnp.int32, (128, 128), 1)
    pick = [
        jnp.where(rows == lanes % 32 + 32 * c, 1.0, 0.0).astype(BF) for c in range(4)
    ]
    for m in range(BLOCKS):
        at = C_AT + 32 * (m // 4)
        for j in range(4):
            block = msg_ref[4 * j : 4 * j + 4, at : at + 32, :].reshape(128, 128)
            spread = dot_nn(block, pick[m % 4])
            bd_ref[m, j] = jnp.where(same, spread, 0.0).astype(BF)
    for ref, first, tiles in (
        (d0_ref, D0_AT, D0_TILES),
        (d1_ref, D1_AT, D1_TILES),
        (d2_ref, D2_AT, D2_TILES),
    ):
        for tile in range(tiles):
            at = first + 32 * tile
            ref[:, 128 * tile : 128 * tile + 128] = msg_ref[:, at : at + 32, :].reshape(512, 128)
    y0 = dot_nt(b_ref[0].astype(BF), d0_ref[...]).astype(BF)
    y0_ref[...] = y0
    for i in range(2):
        mine = jnp.where(leaf % 2 == i, b_ref[1], 0.0)
        p1_ref[:, 512 * i : 512 * i + 512] = (couple([(y0, i)], bd_ref) + mine).astype(BF)


def times_rows(z, d_ref, width):
    total = jnp.zeros((8, 512), F32)
    for at in range(0, width, 1024):
        total = total + dot_nt(z[:, at : at + 1024], d_ref[:, at : at + 1024])
    return total


def forward_kernel(level, leaf_ref, own_ref, other_ref, d_ref, b_ref, bd_ref, *rest):
    ys, (y_ref, p_ref) = rest[:-2], rest[-2:]
    leaf = leaf_ref[0]
    z = (own_ref[...].astype(F32) + other_ref[...].astype(F32)).astype(BF)
    y = times_rows(z, d_ref, z.shape[1]).astype(BF)
    y_ref[...] = y
    vectors = [r[...] for r in ys] + [y]
    span = 2 ** (level + 1)
    for i in range(span):
        mine = jnp.where(leaf % span == i, b_ref[level + 1], 0.0)
        parts = [(vec, OFFSET[level + 1, u] + i) for u, vec in enumerate(vectors)]
        p_ref[:, 512 * i : 512 * i + 512] = (couple(parts, bd_ref) + mine).astype(BF)


def top_kernel(own_ref, other_ref, *rest):
    pieces, x_ref = rest[:-1], rest[-1]

    def rows(at):
        return jnp.concatenate([p[:, at : at + 512] for p in pieces], 0)

    z = (own_ref[...].astype(F32) + other_ref[...].astype(F32)).astype(BF)
    y = jnp.zeros((8, 512), F32)
    for at in range(0, 4096, 512):
        y = y + dot_nt(z[:, at : at + 512], rows(at))
    y = y.astype(BF)
    for at in range(0, 4096, 512):
        x_ref[:, at : at + 512] = dot_nn(y, rows(at)).astype(BF)


def back_kernel(level, leaf_ref, own_ref, other_ref, d_ref, y_ref, bd_ref, *rest):
    first = level == 2
    pending = () if first else rest[: level + 1]
    outs = rest[len(pending) :]
    x_ref, xp_ref, next_refs = outs[0], outs[1], outs[2:]
    leaf = leaf_ref[0]
    span = 2 ** (level + 1)
    total = own_ref[...].astype(F32) + other_ref[...].astype(F32)
    x = total.astype(BF)
    mine = total[:, 0:512]
    for i in range(1, span):
        mine = jnp.where(leaf % span == i, total[:, 512 * i : 512 * i + 512], mine)
    x_ref[...] = mine
    for u in range(level + 1):
        columns = []
        for j in range(4):
            term = None
            for i in range(span):
                at = 512 * i + 128 * j
                part = dot_nn(x[:, at : at + 128], bd_ref[OFFSET[level + 1, u] + i, j])
                term = part if term is None else term + part
            columns.append(term)
        p = jnp.concatenate(columns, 1)
        if not first:
            p = p + pending[u][...]
        if u < level:
            next_refs[u][...] = p
        else:
            q = (y_ref[...].astype(F32) - p).astype(BF)
    if level > 0:
        width = 512 * 2**level
        for at in range(0, width, 1024):
            xp_ref[:, at : at + 1024] = dot_nn(q, d_ref[:, at : at + 1024]).astype(BF)
    else:
        xp_ref[...] = dot_nn(q, d_ref[...])


def pack_kernel(x0_ref, x1_ref, x2_ref, x3_ref, out_ref):
    chunk = lane_chunk(8)
    tiles = [r[:, 128 * j : 128 * j + 128] for r in (x0_ref, x1_ref, x2_ref, x3_ref) for j in range(4)]
    rolled = Rolled(tiles)
    for t in range(16):
        parts = [rolled.take(4 * v + t // 4, t % 4, v) for v in range(4)]
        out_ref[t] = merge(parts, chunk)


def shape(dims, kind=BF):
    return jax.ShapeDtypeStruct(dims, kind)


def reduce_over(part, level):
    hops = [
        [(i, i ^ 1) for i in range(8)],
        [(i, i ^ 2) for i in range(8)],
        [(i, (3 - i // 2) * 2 + i % 2) for i in range(8)],
    ]
    for n in range(level):
        other = lax.ppermute(part, "leaf", hops[n])
        if n == level - 1:
            return part, other
        part = (part.astype(F32) + other.astype(F32)).astype(BF)


def shift_x(values, by):
    return lax.ppermute(values, "tile", [(t, t // 4 * 4 + (t + by) % 4) for t in range(16)])


def shift_z(values, by):
    return lax.ppermute(values, "tile", [(t, (t + 4 * by) % 16) for t in range(16)])


def local(right_sides, diag_inverse, coupling, pattern):
    leaf = lax.axis_index("leaf").astype(jnp.int32).reshape(1)
    upper, lower = diag_inverse[0:16, 3584:], diag_inverse[16:32, 3584:]
    upper = [upper] + [shift_x(upper, k) for k in (1, 2, 3)]
    lower = [lower] + [shift_z(lower, k) for k in (1, 2, 3)]
    upper, lower = jnp.concatenate(upper, 0), jnp.concatenate(lower, 0)
    split = pl.pallas_call(
        split_kernel,
        out_shape=shape((8, 32, 256)),
        in_specs=[VMEM, SMEM],
        out_specs=VMEM,
        compiler_params=params(),
        name="split_couplings",
    )(coupling, pattern)
    columns = lax.all_to_all(split, "leaf", 0, 0, tiled=True)
    message_call = pl.pallas_call(
        message_kernel,
        out_shape=shape((16, MESSAGE, 128)),
        grid=(1,),
        in_specs=[
            SMEM,
            pl.BlockSpec((8, 32, 256), lambda i: (0, 0, 0)),
            pl.BlockSpec((4, 32, 128), lambda i: (0, 0, 0)),
            pl.BlockSpec((32, 3584), lambda i: (0, 0)),
        ],
        out_specs=pl.BlockSpec((16, MESSAGE, 128), lambda i: (0, 0, 0)),
        compiler_params=params(),
        name="message",
    )
    message = message_call(leaf, columns, right_sides, diag_inverse)
    message = lax.all_to_all(message, "tile", 0, 0, tiled=True)
    upper, lower, message = lax.optimization_barrier((upper, lower, message))
    pieces = [upper] + [shift_z(upper, k) for k in (1, 2, 3)]
    pieces += [lower] + [shift_x(lower, k) for k in (1, 2, 3)]
    first_call = pl.pallas_call(
        first_kernel,
        out_shape=(
            shape((4, 8, 512), F32),
            shape((BLOCKS, 4, 128, 128)),
            shape((512, 512)),
            shape((512, 1024)),
            shape((512, 2048)),
            shape((8, 512)),
            shape((8, 1024)),
        ),
        in_specs=[SMEM, VMEM],
        out_specs=(VMEM,) * 7,
        compiler_params=params(),
        name="level0",
    )
    b, bd, d0, d1, d2, y0, p1 = first_call(leaf, message)

    def forward(level, part, d, ys):
        own, other = reduce_over(part, level)
        return pl.pallas_call(
            functools.partial(forward_kernel, level),
            out_shape=(shape((8, 512)), shape((8, 512 * 2 ** (level + 1)))),
            in_specs=[SMEM] + [VMEM] * (5 + len(ys)),
            out_specs=(VMEM,) * 2,
            compiler_params=params(),
        )(leaf, own, other, d, b, bd, *ys)

    y1, p2 = forward(1, p1, d1, (y0,))
    y2, p3 = forward(2, p2, d2, (y0, y1))
    own, other = reduce_over(p3, 3)
    xp = pl.pallas_call(
        top_kernel,
        out_shape=shape((8, 4096)),
        in_specs=[VMEM] * 10,
        out_specs=VMEM,
        compiler_params=params(),
        name="level3",
    )(own, other, *pieces)

    def back(level, part, d, y, pending):
        own, other = reduce_over(part, level + 1)
        out = [shape((8, 512), F32)]
        out.append(shape((8, 512 * 2**level), BF if level else F32))
        out += [shape((8, 512), F32)] * level
        return pl.pallas_call(
            functools.partial(back_kernel, level),
            out_shape=tuple(out),
            in_specs=[SMEM] + [VMEM] * (5 + len(pending)),
            out_specs=(VMEM,) * len(out),
            compiler_params=params(),
        )(leaf, own, other, d, y, bd, *pending)

    x3, xp, *pending = back(2, xp, d2, y2, ())
    x2, xp, *pending = back(1, xp, d1, y1, pending)
    x1, x0 = back(0, xp, d0, y0, pending)
    packed = pl.pallas_call(
        pack_kernel,
        out_shape=shape((16, 8, 128), F32),
        in_specs=[VMEM] * 4,
        out_specs=VMEM,
        compiler_params=params(),
        name="pack",
    )(x0, x1, x2, x3)
    packed = lax.all_to_all(packed, "tile", 0, 0, tiled=True)
    return jnp.transpose(packed.reshape(128, 128)).reshape(4, 32, 128)


def solution(mesh):
    placed = (
        P(None, ("leaf", "tile"), None),
        P(("leaf", "tile"), None),
        P(("leaf", "tile"), None),
        P(("leaf", "tile"), None),
    )
    return jax.shard_map(
        local,
        mesh=mesh,
        in_specs=placed,
        out_specs=P(None, ("leaf", "tile"), None),
        check_vma=False,
    )
```

```python
import functools

import jax
import jax.numpy as jnp
from jax import lax
from jax.experimental import pallas as pl
from jax.experimental.pallas import tpu as pltpu
from jax.sharding import PartitionSpec as P


BF = jnp.bfloat16
F32 = jnp.float32
PAIRS = ((1, 0), (2, 0), (2, 1), (3, 0), (3, 1), (3, 2))
OFFSET = {(1, 0): 0, (2, 0): 2, (2, 1): 6, (3, 0): 10, (3, 1): 18, (3, 2): 26}
BLOCKS = 34
VMEM = pl.BlockSpec(memory_space=pltpu.VMEM)
SMEM = pl.BlockSpec(memory_space=pltpu.SMEM)
RHS_ROWS, C_TILES, D0_TILES, D1_TILES = 16, 9, 4, 8
C_AT = RHS_ROWS
D0_AT = C_AT + 32 * C_TILES
D1_AT = D0_AT + 32 * D0_TILES
MESSAGE = D1_AT + 32 * D1_TILES


def params(mib=48):
    return pltpu.CompilerParams(vmem_limit_bytes=mib * 2**20)


def lane_chunk(rows):
    return lax.broadcasted_iota(jnp.int32, (rows, 128), 1) // 32


def dot_nt(a, b):
    return lax.dot_general(a, b, (((1,), (1,)), ((), ())), preferred_element_type=F32)


def dot_nn(a, b):
    return jnp.dot(a, b, preferred_element_type=F32)


class Rolled:
    def __init__(self, tiles):
        self.tiles = tiles
        self.made = {}

    def take(self, tile, source, target):
        shift = (target - source) % 4 * 32
        if shift == 0:
            return self.tiles[tile]
        if (tile, shift) not in self.made:
            self.made[tile, shift] = pltpu.roll(self.tiles[tile], shift, 1)
        return self.made[tile, shift]


def merge(parts, chunk):
    result = parts[0]
    for c in range(1, len(parts)):
        result = jnp.where(chunk == c, parts[c], result)
    return result


def split_kernel(coupling_ref, pattern_ref, out_ref):
    chunk = lane_chunk(32)
    tiles = []
    for tile in range(C_TILES):
        if tile < 8:
            values = coupling_ref[:, 128 * tile : 128 * tile + 128].astype(F32)
        else:
            half = coupling_ref[:, 1024:1088].astype(F32)
            values = jnp.concatenate([half, jnp.zeros_like(half)], 1)
        keep = jnp.zeros((32, 128), F32)
        for c in range(4):
            if 4 * tile + c < BLOCKS:
                keep = jnp.where(chunk == c, pattern_ref[0, 4 * tile + c].astype(F32), keep)
        tiles.append(values * keep)
    rolled = Rolled(tiles)
    for leaf in range(8):
        parts = []
        for q, (w, u) in enumerate(PAIRS):
            block = OFFSET[w, u] + leaf % 2**w
            parts.append(rolled.take(block // 4, block % 4, q % 4))
        out_ref[leaf, :, 0:128] = merge(parts[:4], chunk).astype(BF)
        out_ref[leaf, :, 128:256] = merge(parts[4:], chunk).astype(BF)


def message_kernel(leaf_ref, columns_ref, rhs_ref, diag_ref, out_ref):
    leaf = leaf_ref[0]
    chunk = lane_chunk(32)
    common = []
    sources = []
    for w, u in PAIRS:
        q = PAIRS.index((w, u))
        for i in range(2**w):
            sources.append((leaf // 2**w * 2**w + i, q))
    for tile in range(C_TILES):
        parts = []
        for c in range(4):
            if 4 * tile + c < BLOCKS:
                source, q = sources[4 * tile + c]
                values = columns_ref[source, :, 128 * (q // 4) : 128 * (q // 4) + 128].astype(F32)
                shift = (c - q) % 4 * 32
                parts.append(values if shift == 0 else pltpu.roll(values, shift, 1))
        common.append(merge(parts, chunk).astype(BF))
    for tile in range(D0_TILES + D1_TILES):
        common.append(diag_ref[:, 128 * tile : 128 * tile + 128])
    rhs = jnp.transpose(rhs_ref[...].reshape(128, 128))
    high = rhs.astype(BF).astype(F32)
    low = rhs - high
    for tile in range(16):
        both = jnp.concatenate([high[8 * tile : 8 * tile + 8], low[8 * tile : 8 * tile + 8]], 0)
        out_ref[tile, 0:RHS_ROWS] = both.astype(BF)
        for n, values in enumerate(common):
            out_ref[tile, C_AT + 32 * n : C_AT + 32 * n + 32] = values


def couple(parts, bd_ref):
    out = []
    for j in range(4):
        total = None
        for vector, m in parts:
            term = dot_nt(vector[:, 128 * j : 128 * j + 128], bd_ref[m, j])
            total = term if total is None else total + term
        out.append(-total)
    return jnp.concatenate(out, 1)


def first_kernel(leaf_ref, msg_ref, b_ref, bd_ref, d0_ref, d1_ref, y0_ref, p1_ref):
    leaf = leaf_ref[0]
    chunk8 = lane_chunk(8)
    rhs = Rolled(
        [msg_ref[t, 0:8].astype(F32) + msg_ref[t, 8:16].astype(F32) for t in range(16)]
    )
    for v in range(4):
        for j in range(4):
            parts = [rhs.take(4 * j + c, v, c) for c in range(4)]
            b_ref[v, :, 128 * j : 128 * j + 128] = merge(parts, chunk8)
    row_chunk = lax.broadcasted_iota(jnp.int32, (128, 128), 0) // 32
    same = row_chunk == lane_chunk(128)
    rows = lax.broadcasted_iota(jnp.int32, (128, 128), 0)
    lanes = lax.broadcasted_iota(jnp.int32, (128, 128), 1)
    pick = [
        jnp.where(rows == lanes % 32 + 32 * c, 1.0, 0.0).astype(BF) for c in range(4)
    ]
    for m in range(BLOCKS):
        at = C_AT + 32 * (m // 4)
        for j in range(4):
            block = msg_ref[4 * j : 4 * j + 4, at : at + 32, :].reshape(128, 128)
            spread = dot_nn(block, pick[m % 4])
            bd_ref[m, j] = jnp.where(same, spread, 0.0).astype(BF)
    for ref, first, tiles in (
        (d0_ref, D0_AT, D0_TILES),
        (d1_ref, D1_AT, D1_TILES),
    ):
        for tile in range(tiles):
            at = first + 32 * tile
            ref[:, 128 * tile : 128 * tile + 128] = msg_ref[:, at : at + 32, :].reshape(512, 128)
    y0 = dot_nt(b_ref[0].astype(BF), d0_ref[...]).astype(BF)
    y0_ref[...] = y0
    for i in range(2):
        mine = jnp.where(leaf % 2 == i, b_ref[1], 0.0)
        p1_ref[:, 512 * i : 512 * i + 512] = (couple([(y0, i)], bd_ref) + mine).astype(BF)


def times_rows(z, d_ref, width):
    total = jnp.zeros((8, 512), F32)
    for at in range(0, width, 1024):
        total = total + dot_nt(z[:, at : at + 1024], d_ref[:, at : at + 1024])
    return total


def order_kernel(place_ref, *rest):
    pieces, d_ref = rest[:-1], rest[-1]
    z, x = place_ref[0] // 4, place_ref[0] % 4
    for half in range(2):
        for n in range(4):
            for m in range(4):
                dz, dx = (n, m) if half == 0 else (m, n)
                tile = (z - dz + 4) % 4 * 4 + (x - dx + 4) % 4
                at = pl.multiple_of(tile * 32 + 16 * half, 16)
                d_ref[pl.ds(at, 16), :] = pieces[4 * half + n][16 * m : 16 * m + 16, :]


def forward_kernel(level, leaf_ref, own_ref, other_ref, d_ref, b_ref, bd_ref, *rest):
    ys, (y_ref, p_ref) = rest[:-2], rest[-2:]
    leaf = leaf_ref[0]
    z = (own_ref[...].astype(F32) + other_ref[...].astype(F32)).astype(BF)
    y = times_rows(z, d_ref, z.shape[1]).astype(BF)
    y_ref[...] = y
    vectors = [r[...] for r in ys] + [y]
    span = 2 ** (level + 1)
    for i in range(span):
        mine = jnp.where(leaf % span == i, b_ref[level + 1], 0.0)
        parts = [(vec, OFFSET[level + 1, u] + i) for u, vec in enumerate(vectors)]
        p_ref[:, 512 * i : 512 * i + 512] = (couple(parts, bd_ref) + mine).astype(BF)


def top_kernel(own_ref, other_ref, *rest):
    pieces, x_ref = rest[:-1], rest[-1]

    def rows(at):
        return jnp.concatenate([p[:, at : at + 512] for p in pieces], 0)

    z = (own_ref[...].astype(F32) + other_ref[...].astype(F32)).astype(BF)
    y = jnp.zeros((8, 512), F32)
    for at in range(0, 4096, 512):
        y = y + dot_nt(z[:, at : at + 512], rows(at))
    y = y.astype(BF)
    for at in range(0, 4096, 512):
        x_ref[:, at : at + 512] = dot_nn(y, rows(at)).astype(BF)


def back_kernel(level, leaf_ref, own_ref, other_ref, d_ref, y_ref, bd_ref, *rest):
    first = level == 2
    pending = () if first else rest[: level + 1]
    outs = rest[len(pending) :]
    x_ref, xp_ref, next_refs = outs[0], outs[1], outs[2:]
    leaf = leaf_ref[0]
    span = 2 ** (level + 1)
    total = own_ref[...].astype(F32) + other_ref[...].astype(F32)
    x = total.astype(BF)
    mine = total[:, 0:512]
    for i in range(1, span):
        mine = jnp.where(leaf % span == i, total[:, 512 * i : 512 * i + 512], mine)
    x_ref[...] = mine
    for u in range(level + 1):
        columns = []
        for j in range(4):
            term = None
            for i in range(span):
                at = 512 * i + 128 * j
                part = dot_nn(x[:, at : at + 128], bd_ref[OFFSET[level + 1, u] + i, j])
                term = part if term is None else term + part
            columns.append(term)
        p = jnp.concatenate(columns, 1)
        if not first:
            p = p + pending[u][...]
        if u < level:
            next_refs[u][...] = p
        else:
            q = (y_ref[...].astype(F32) - p).astype(BF)
    if level > 0:
        width = 512 * 2**level
        for at in range(0, width, 1024):
            xp_ref[:, at : at + 1024] = dot_nn(q, d_ref[:, at : at + 1024]).astype(BF)
    else:
        xp_ref[...] = dot_nn(q, d_ref[...])


def pack_kernel(x0_ref, x1_ref, x2_ref, x3_ref, out_ref):
    chunk = lane_chunk(8)
    tiles = [r[:, 128 * j : 128 * j + 128] for r in (x0_ref, x1_ref, x2_ref, x3_ref) for j in range(4)]
    rolled = Rolled(tiles)
    for t in range(16):
        parts = [rolled.take(4 * v + t // 4, t % 4, v) for v in range(4)]
        out_ref[t] = merge(parts, chunk)


def shape(dims, kind=BF):
    return jax.ShapeDtypeStruct(dims, kind)


def reduce_over(part, level):
    hops = [
        [(i, i ^ 1) for i in range(8)],
        [(i, i ^ 2) for i in range(8)],
        [(i, (3 - i // 2) * 2 + i % 2) for i in range(8)],
    ]
    for n in range(level):
        other = lax.ppermute(part, "leaf", hops[n])
        if n == level - 1:
            return part, other
        part = (part.astype(F32) + other.astype(F32)).astype(BF)


def shift_x(values, by):
    return lax.ppermute(values, "tile", [(t, t // 4 * 4 + (t + by) % 4) for t in range(16)])


def shift_z(values, by):
    return lax.ppermute(values, "tile", [(t, (t + 4 * by) % 16) for t in range(16)])


def local(right_sides, diag_inverse, coupling, pattern):
    leaf = lax.axis_index("leaf").astype(jnp.int32).reshape(1)
    upper, lower = diag_inverse[0:16, 1536:], diag_inverse[16:32, 1536:]
    upper = [upper] + [shift_x(upper, k) for k in (1, 2, 3)]
    lower = [lower] + [shift_z(lower, k) for k in (1, 2, 3)]

    def joined(parts, first, stop):
        return jnp.concatenate([p[:, first:stop] for p in parts], 0)

    def far(upper, lower):
        pieces = [upper] + [shift_z(upper, k) for k in (1, 2, 3)]
        return pieces + [lower] + [shift_x(lower, k) for k in (1, 2, 3)]

    pieces2 = far(joined(upper, 0, 2048), joined(lower, 0, 2048))
    upper, lower = joined(upper, 2048, 6144), joined(lower, 2048, 6144)
    split = pl.pallas_call(
        split_kernel,
        out_shape=shape((8, 32, 256)),
        in_specs=[VMEM, SMEM],
        out_specs=VMEM,
        compiler_params=params(),
        name="split_couplings",
    )(coupling, pattern)
    columns = lax.all_to_all(split, "leaf", 0, 0, tiled=True)
    message_call = pl.pallas_call(
        message_kernel,
        out_shape=shape((16, MESSAGE, 128)),
        grid=(1,),
        in_specs=[
            SMEM,
            pl.BlockSpec((8, 32, 256), lambda i: (0, 0, 0)),
            pl.BlockSpec((4, 32, 128), lambda i: (0, 0, 0)),
            pl.BlockSpec((32, 1536), lambda i: (0, 0)),
        ],
        out_specs=pl.BlockSpec((16, MESSAGE, 128), lambda i: (0, 0, 0)),
        compiler_params=params(),
        name="message",
    )
    message = message_call(leaf, columns, right_sides, diag_inverse)
    message = lax.all_to_all(message, "tile", 0, 0, tiled=True)
    upper, lower, message = lax.optimization_barrier((upper, lower, message))
    pieces3 = far(upper, lower)
    first_call = pl.pallas_call(
        first_kernel,
        out_shape=(
            shape((4, 8, 512), F32),
            shape((BLOCKS, 4, 128, 128)),
            shape((512, 512)),
            shape((512, 1024)),
            shape((8, 512)),
            shape((8, 1024)),
        ),
        in_specs=[SMEM, VMEM],
        out_specs=(VMEM,) * 6,
        compiler_params=params(),
        name="level0",
    )
    b, bd, d0, d1, y0, p1 = first_call(leaf, message)

    place = lax.axis_index("tile").astype(jnp.int32).reshape(1)
    order_call = pl.pallas_call(
        order_kernel,
        out_shape=shape((512, 2048)),
        in_specs=[SMEM] + [VMEM] * 8,
        out_specs=VMEM,
        compiler_params=params(),
        name="order2",
    )
    d2 = order_call(place, *pieces2)

    def forward(level, part, d, ys):
        own, other = reduce_over(part, level)
        return pl.pallas_call(
            functools.partial(forward_kernel, level),
            out_shape=(shape((8, 512)), shape((8, 512 * 2 ** (level + 1)))),
            in_specs=[SMEM] + [VMEM] * (5 + len(ys)),
            out_specs=(VMEM,) * 2,
            compiler_params=params(),
        )(leaf, own, other, d, b, bd, *ys)

    y1, p2 = forward(1, p1, d1, (y0,))
    y2, p3 = forward(2, p2, d2, (y0, y1))
    own, other = reduce_over(p3, 3)
    xp = pl.pallas_call(
        top_kernel,
        out_shape=shape((8, 4096)),
        in_specs=[VMEM] * 10,
        out_specs=VMEM,
        compiler_params=params(),
        name="level3",
    )(own, other, *pieces3)

    def back(level, part, d, y, pending):
        own, other = reduce_over(part, level + 1)
        out = [shape((8, 512), F32)]
        out.append(shape((8, 512 * 2**level), BF if level else F32))
        out += [shape((8, 512), F32)] * level
        return pl.pallas_call(
            functools.partial(back_kernel, level),
            out_shape=tuple(out),
            in_specs=[SMEM] + [VMEM] * (5 + len(pending)),
            out_specs=(VMEM,) * len(out),
            compiler_params=params(),
        )(leaf, own, other, d, y, bd, *pending)

    x3, xp, *pending = back(2, xp, d2, y2, ())
    x2, xp, *pending = back(1, xp, d1, y1, pending)
    x1, x0 = back(0, xp, d0, y0, pending)
    packed = pl.pallas_call(
        pack_kernel,
        out_shape=shape((16, 8, 128), F32),
        in_specs=[VMEM] * 4,
        out_specs=VMEM,
        compiler_params=params(),
        name="pack",
    )(x0, x1, x2, x3)
    packed = lax.all_to_all(packed, "tile", 0, 0, tiled=True)
    return jnp.transpose(packed.reshape(128, 128)).reshape(4, 32, 128)


def solution(mesh):
    placed = (
        P(None, ("leaf", "tile"), None),
        P(("leaf", "tile"), None),
        P(("leaf", "tile"), None),
        P(("leaf", "tile"), None),
    )
    return jax.shard_map(
        local,
        mesh=mesh,
        in_specs=placed,
        out_specs=P(None, ("leaf", "tile"), None),
        check_vma=False,
    )
```

```python
import functools

import jax
import jax.numpy as jnp
from jax import lax
from jax.experimental import pallas as pl
from jax.experimental.pallas import tpu as pltpu
from jax.sharding import PartitionSpec as P


BF = jnp.bfloat16
F32 = jnp.float32
PAIRS = ((1, 0), (2, 0), (2, 1), (3, 0), (3, 1), (3, 2))
OFFSET = {(1, 0): 0, (2, 0): 2, (2, 1): 6, (3, 0): 10, (3, 1): 18, (3, 2): 26}
BLOCKS = 34
VMEM = pl.BlockSpec(memory_space=pltpu.VMEM)
SMEM = pl.BlockSpec(memory_space=pltpu.SMEM)
RHS_ROWS, C_TILES = 16, 9
C_AT = RHS_ROWS
MESSAGE = C_AT + 32 * C_TILES


def params(mib=20):
    return pltpu.CompilerParams(vmem_limit_bytes=mib * 2**20)


def lane_chunk(rows):
    return lax.broadcasted_iota(jnp.int32, (rows, 128), 1) // 32


def dot_nt(a, b):
    return lax.dot_general(a, b, (((1,), (1,)), ((), ())), preferred_element_type=F32)


def dot_nn(a, b):
    return jnp.dot(a, b, preferred_element_type=F32)


class Rolled:
    def __init__(self, tiles):
        self.tiles = tiles
        self.made = {}

    def take(self, tile, source, target):
        shift = (target - source) % 4 * 32
        if shift == 0:
            return self.tiles[tile]
        if (tile, shift) not in self.made:
            self.made[tile, shift] = pltpu.roll(self.tiles[tile], shift, 1)
        return self.made[tile, shift]


def merge(parts, chunk):
    result = parts[0]
    for c in range(1, len(parts)):
        result = jnp.where(chunk == c, parts[c], result)
    return result


def split_kernel(coupling_ref, pattern_ref, out_ref):
    chunk = lane_chunk(32)
    tiles = []
    for tile in range(C_TILES):
        if tile < 8:
            values = coupling_ref[:, 128 * tile : 128 * tile + 128].astype(F32)
        else:
            half = coupling_ref[:, 1024:1088].astype(F32)
            values = jnp.concatenate([half, jnp.zeros_like(half)], 1)
        keep = jnp.zeros((32, 128), F32)
        for c in range(4):
            if 4 * tile + c < BLOCKS:
                keep = jnp.where(chunk == c, pattern_ref[0, 4 * tile + c].astype(F32), keep)
        tiles.append(values * keep)
    rolled = Rolled(tiles)
    for leaf in range(8):
        parts = []
        for q, (w, u) in enumerate(PAIRS):
            block = OFFSET[w, u] + leaf % 2**w
            parts.append(rolled.take(block // 4, block % 4, q % 4))
        out_ref[leaf, :, 0:128] = merge(parts[:4], chunk).astype(BF)
        out_ref[leaf, :, 128:256] = merge(parts[4:], chunk).astype(BF)


def message_kernel(leaf_ref, columns_ref, rhs_ref, out_ref):
    leaf = leaf_ref[0]
    chunk = lane_chunk(32)
    common = []
    sources = []
    for w, u in PAIRS:
        q = PAIRS.index((w, u))
        for i in range(2**w):
            sources.append((leaf // 2**w * 2**w + i, q))
    for tile in range(C_TILES):
        parts = []
        for c in range(4):
            if 4 * tile + c < BLOCKS:
                source, q = sources[4 * tile + c]
                values = columns_ref[source, :, 128 * (q // 4) : 128 * (q // 4) + 128].astype(F32)
                shift = (c - q) % 4 * 32
                parts.append(values if shift == 0 else pltpu.roll(values, shift, 1))
        common.append(merge(parts, chunk).astype(BF))
    rhs = jnp.transpose(rhs_ref[...].reshape(128, 128))
    high = rhs.astype(BF).astype(F32)
    low = rhs - high
    for tile in range(16):
        both = jnp.concatenate([high[8 * tile : 8 * tile + 8], low[8 * tile : 8 * tile + 8]], 0)
        out_ref[tile, 0:RHS_ROWS] = both.astype(BF)
        for n, values in enumerate(common):
            out_ref[tile, C_AT + 32 * n : C_AT + 32 * n + 32] = values


def couple(parts, bd_ref):
    out = []
    for j in range(4):
        total = None
        for vector, m in parts:
            term = dot_nt(vector[:, 128 * j : 128 * j + 128], bd_ref[m, j])
            total = term if total is None else total + term
        out.append(-total)
    return jnp.concatenate(out, 1)


def put_in_order(place_ref, pieces, refs):
    z, x = place_ref[0] // 4, place_ref[0] % 4
    for half in range(2):
        for n in range(4):
            for m in range(4):
                dz, dx = (n, m) if half == 0 else (m, n)
                tile = (z - dz + 4) % 4 * 4 + (x - dx + 4) % 4
                at = pl.multiple_of(tile * 32 + 16 * half, 16)
                first = 0
                for ref in refs:
                    last = first + ref.shape[1]
                    rows = pieces[4 * half + n][16 * m : 16 * m + 16, first:last]
                    ref[pl.ds(at, 16), :] = rows
                    first = last


def order_kernel(place_ref, *rest):
    put_in_order(place_ref, rest[:-1], rest[-1:])


def stack_kernel(*refs):
    parts, outs = refs[:4], refs[4:]
    first = 0
    for out in outs:
        last = first + out.shape[1]
        for n, part in enumerate(parts):
            out[16 * n : 16 * n + 16, :] = part[:, first:last]
        first = last


def first_kernel(leaf_ref, place_ref, msg_ref, *rest):
    pieces, outs = rest[:8], rest[8:]
    b_ref, bd_ref, d0_ref, d1_ref, y0_ref, p1_ref = outs
    leaf = leaf_ref[0]
    chunk8 = lane_chunk(8)
    rhs = Rolled(
        [msg_ref[t, 0:8].astype(F32) + msg_ref[t, 8:16].astype(F32) for t in range(16)]
    )
    for v in range(4):
        for j in range(4):
            parts = [rhs.take(4 * j + c, v, c) for c in range(4)]
            b_ref[v, :, 128 * j : 128 * j + 128] = merge(parts, chunk8)
    row_chunk = lax.broadcasted_iota(jnp.int32, (128, 128), 0) // 32
    same = row_chunk == lane_chunk(128)
    rows = lax.broadcasted_iota(jnp.int32, (128, 128), 0)
    lanes = lax.broadcasted_iota(jnp.int32, (128, 128), 1)
    pick = [
        jnp.where(rows == lanes % 32 + 32 * c, 1.0, 0.0).astype(BF) for c in range(4)
    ]
    for m in range(BLOCKS):
        at = C_AT + 32 * (m // 4)
        for j in range(4):
            block = msg_ref[4 * j : 4 * j + 4, at : at + 32, :].reshape(128, 128)
            spread = dot_nn(block, pick[m % 4])
            bd_ref[m, j] = jnp.where(same, spread, 0.0).astype(BF)
    put_in_order(place_ref, pieces, (d0_ref, d1_ref))
    y0 = dot_nt(b_ref[0].astype(BF), d0_ref[...]).astype(BF)
    y0_ref[...] = y0
    for i in range(2):
        mine = jnp.where(leaf % 2 == i, b_ref[1], 0.0)
        p1_ref[:, 512 * i : 512 * i + 512] = (couple([(y0, i)], bd_ref) + mine).astype(BF)


def times_rows(z, d_ref, width):
    total = jnp.zeros((8, 512), F32)
    for at in range(0, width, 1024):
        total = total + dot_nt(z[:, at : at + 1024], d_ref[:, at : at + 1024])
    return total


def forward_kernel(level, leaf_ref, own_ref, other_ref, d_ref, b_ref, bd_ref, *rest):
    ys, (y_ref, p_ref) = rest[:-2], rest[-2:]
    leaf = leaf_ref[0]
    z = (own_ref[...].astype(F32) + other_ref[...].astype(F32)).astype(BF)
    y = times_rows(z, d_ref, z.shape[1]).astype(BF)
    y_ref[...] = y
    vectors = [r[...] for r in ys] + [y]
    span = 2 ** (level + 1)
    for i in range(span):
        mine = jnp.where(leaf % span == i, b_ref[level + 1], 0.0)
        parts = [(vec, OFFSET[level + 1, u] + i) for u, vec in enumerate(vectors)]
        p_ref[:, 512 * i : 512 * i + 512] = (couple(parts, bd_ref) + mine).astype(BF)


def top_kernel(own_ref, other_ref, *rest):
    pieces, x_ref = rest[:-1], rest[-1]

    def rows(at):
        return jnp.concatenate([p[:, at : at + 512] for p in pieces], 0)

    z = (own_ref[...].astype(F32) + other_ref[...].astype(F32)).astype(BF)
    y = jnp.zeros((8, 512), F32)
    for at in range(0, 4096, 512):
        y = y + dot_nt(z[:, at : at + 512], rows(at))
    y = y.astype(BF)
    for at in range(0, 4096, 512):
        x_ref[:, at : at + 512] = dot_nn(y, rows(at)).astype(BF)


def back_kernel(level, leaf_ref, own_ref, other_ref, d_ref, y_ref, bd_ref, *rest):
    first = level == 2
    pending = () if first else rest[: level + 1]
    outs = rest[len(pending) :]
    x_ref, xp_ref, next_refs = outs[0], outs[1], outs[2:]
    leaf = leaf_ref[0]
    span = 2 ** (level + 1)
    total = own_ref[...].astype(F32) + other_ref[...].astype(F32)
    x = total.astype(BF)
    mine = total[:, 0:512]
    for i in range(1, span):
        mine = jnp.where(leaf % span == i, total[:, 512 * i : 512 * i + 512], mine)
    x_ref[...] = mine
    for u in range(level + 1):
        columns = []
        for j in range(4):
            term = None
            for i in range(span):
                at = 512 * i + 128 * j
                part = dot_nn(x[:, at : at + 128], bd_ref[OFFSET[level + 1, u] + i, j])
                term = part if term is None else term + part
            columns.append(term)
        p = jnp.concatenate(columns, 1)
        if not first:
            p = p + pending[u][...]
        if u < level:
            next_refs[u][...] = p
        else:
            q = (y_ref[...].astype(F32) - p).astype(BF)
    if level > 0:
        width = 512 * 2**level
        for at in range(0, width, 1024):
            xp_ref[:, at : at + 1024] = dot_nn(q, d_ref[:, at : at + 1024]).astype(BF)
    else:
        xp_ref[...] = dot_nn(q, d_ref[...])


def pack_kernel(x0_ref, x1_ref, x2_ref, x3_ref, out_ref):
    chunk = lane_chunk(8)
    tiles = [r[:, 128 * j : 128 * j + 128] for r in (x0_ref, x1_ref, x2_ref, x3_ref) for j in range(4)]
    rolled = Rolled(tiles)
    for t in range(16):
        parts = [rolled.take(4 * v + t // 4, t % 4, v) for v in range(4)]
        out_ref[t] = merge(parts, chunk)


def shape(dims, kind=BF):
    return jax.ShapeDtypeStruct(dims, kind)


def reduce_over(part, level):
    hops = [
        [(i, i ^ 1) for i in range(8)],
        [(i, i ^ 2) for i in range(8)],
        [(i, (3 - i // 2) * 2 + i % 2) for i in range(8)],
    ]
    for n in range(level):
        other = lax.ppermute(part, "leaf", hops[n])
        if n == level - 1:
            return part, other
        part = (part.astype(F32) + other.astype(F32)).astype(BF)


def shift_x(values, by):
    return lax.ppermute(values, "tile", [(t, t // 4 * 4 + (t + by) % 4) for t in range(16)])


def shift_z(values, by):
    return lax.ppermute(values, "tile", [(t, (t + 4 * by) % 16) for t in range(16)])


def local(right_sides, diag_inverse, coupling, pattern):
    leaf = lax.axis_index("leaf").astype(jnp.int32).reshape(1)
    place = lax.axis_index("tile").astype(jnp.int32).reshape(1)
    upper, lower = diag_inverse[0:16], diag_inverse[16:32]
    upper = [upper] + [shift_x(upper, k) for k in (1, 2, 3)]
    lower = [lower] + [shift_z(lower, k) for k in (1, 2, 3)]

    stack = pl.pallas_call(
        stack_kernel,
        out_shape=(shape((64, 1536)), shape((64, 2048)), shape((64, 4096))),
        in_specs=[VMEM] * 4,
        out_specs=(VMEM,) * 3,
        compiler_params=params(),
        name="stack",
    )
    upper1, upper2, upper = stack(*upper)
    lower1, lower2, lower = stack(*lower)

    def far(upper, lower):
        pieces = [upper] + [shift_z(upper, k) for k in (1, 2, 3)]
        return pieces + [lower] + [shift_x(lower, k) for k in (1, 2, 3)]

    pieces1 = far(upper1, lower1)
    pieces2 = far(upper2, lower2)
    split = pl.pallas_call(
        split_kernel,
        out_shape=shape((8, 32, 256)),
        in_specs=[VMEM, SMEM],
        out_specs=VMEM,
        compiler_params=params(),
        name="split_couplings",
    )(coupling, pattern)
    columns = lax.all_to_all(split, "leaf", 0, 0, tiled=True)
    message_call = pl.pallas_call(
        message_kernel,
        out_shape=shape((16, MESSAGE, 128)),
        in_specs=[SMEM, VMEM, VMEM],
        out_specs=VMEM,
        compiler_params=params(),
        name="message",
    )
    message = message_call(leaf, columns, right_sides)
    message = lax.all_to_all(message, "tile", 0, 0, tiled=True)
    upper, lower, message = lax.optimization_barrier((upper, lower, message))
    pieces3 = far(upper, lower)
    first_call = pl.pallas_call(
        first_kernel,
        out_shape=(
            shape((4, 8, 512), F32),
            shape((BLOCKS, 4, 128, 128)),
            shape((512, 512)),
            shape((512, 1024)),
            shape((8, 512)),
            shape((8, 1024)),
        ),
        in_specs=[SMEM, SMEM] + [VMEM] * 9,
        out_specs=(VMEM,) * 6,
        compiler_params=params(),
        name="level0",
    )
    b, bd, d0, d1, y0, p1 = first_call(leaf, place, message, *pieces1)

    order_call = pl.pallas_call(
        order_kernel,
        out_shape=shape((512, 2048)),
        in_specs=[SMEM] + [VMEM] * 8,
        out_specs=VMEM,
        compiler_params=params(),
        name="order2",
    )
    d2 = order_call(place, *pieces2)

    def forward(level, part, d, ys):
        own, other = reduce_over(part, level)
        return pl.pallas_call(
            functools.partial(forward_kernel, level),
            out_shape=(shape((8, 512)), shape((8, 512 * 2 ** (level + 1)))),
            in_specs=[SMEM] + [VMEM] * (5 + len(ys)),
            out_specs=(VMEM,) * 2,
            compiler_params=params(),
        )(leaf, own, other, d, b, bd, *ys)

    y1, p2 = forward(1, p1, d1, (y0,))
    y2, p3 = forward(2, p2, d2, (y0, y1))
    own, other = reduce_over(p3, 3)
    xp = pl.pallas_call(
        top_kernel,
        out_shape=shape((8, 4096)),
        in_specs=[VMEM] * 10,
        out_specs=VMEM,
        compiler_params=params(),
        name="level3",
    )(own, other, *pieces3)

    def back(level, part, d, y, pending):
        own, other = reduce_over(part, level + 1)
        out = [shape((8, 512), F32)]
        out.append(shape((8, 512 * 2**level), BF if level else F32))
        out += [shape((8, 512), F32)] * level
        return pl.pallas_call(
            functools.partial(back_kernel, level),
            out_shape=tuple(out),
            in_specs=[SMEM] + [VMEM] * (5 + len(pending)),
            out_specs=(VMEM,) * len(out),
            compiler_params=params(),
        )(leaf, own, other, d, y, bd, *pending)

    x3, xp, *pending = back(2, xp, d2, y2, ())
    x2, xp, *pending = back(1, xp, d1, y1, pending)
    x1, x0 = back(0, xp, d0, y0, pending)
    packed = pl.pallas_call(
        pack_kernel,
        out_shape=shape((16, 8, 128), F32),
        in_specs=[VMEM] * 4,
        out_specs=VMEM,
        compiler_params=params(),
        name="pack",
    )(x0, x1, x2, x3)
    packed = lax.all_to_all(packed, "tile", 0, 0, tiled=True)
    return jnp.transpose(packed.reshape(128, 128)).reshape(4, 32, 128)


def solution(mesh):
    placed = (
        P(None, ("leaf", "tile"), None),
        P(("leaf", "tile"), None),
        P(("leaf", "tile"), None),
        P(("leaf", "tile"), None),
    )
    return jax.shard_map(
        local,
        mesh=mesh,
        in_specs=placed,
        out_specs=P(None, ("leaf", "tile"), None),
        check_vma=False,
    )
```

```python
import functools

import jax
import jax.numpy as jnp
from jax import lax
from jax.experimental import pallas as pl
from jax.experimental.pallas import tpu as pltpu
from jax.sharding import PartitionSpec as P


BF = jnp.bfloat16
F32 = jnp.float32
PAIRS = ((1, 0), (2, 0), (2, 1), (3, 0), (3, 1), (3, 2))
OFFSET = {(1, 0): 0, (2, 0): 2, (2, 1): 6, (3, 0): 10, (3, 1): 18, (3, 2): 26}
BLOCKS = 34
VMEM = pl.BlockSpec(memory_space=pltpu.VMEM)
SMEM = pl.BlockSpec(memory_space=pltpu.SMEM)
RHS_ROWS, C_TILES = 16, 9
C_AT = RHS_ROWS
MESSAGE = C_AT + 32 * C_TILES


def params(mib=20):
    return pltpu.CompilerParams(vmem_limit_bytes=mib * 2**20)


def lane_chunk(rows):
    return lax.broadcasted_iota(jnp.int32, (rows, 128), 1) // 32


def dot_nt(a, b):
    return lax.dot_general(a, b, (((1,), (1,)), ((), ())), preferred_element_type=F32)


def dot_nn(a, b):
    return jnp.dot(a, b, preferred_element_type=F32)


class Rolled:
    def __init__(self, tiles):
        self.tiles = tiles
        self.made = {}

    def take(self, tile, source, target):
        shift = (target - source) % 4 * 32
        if shift == 0:
            return self.tiles[tile]
        if (tile, shift) not in self.made:
            self.made[tile, shift] = pltpu.roll(self.tiles[tile], shift, 1)
        return self.made[tile, shift]


def merge(parts, chunk):
    result = parts[0]
    for c in range(1, len(parts)):
        result = jnp.where(chunk == c, parts[c], result)
    return result


def split_kernel(coupling_ref, pattern_ref, out_ref):
    chunk = lane_chunk(32)
    tiles = []
    for tile in range(C_TILES):
        if tile < 8:
            values = coupling_ref[:, 128 * tile : 128 * tile + 128].astype(F32)
        else:
            half = coupling_ref[:, 1024:1088].astype(F32)
            values = jnp.concatenate([half, jnp.zeros_like(half)], 1)
        keep = jnp.zeros((32, 128), F32)
        for c in range(4):
            if 4 * tile + c < BLOCKS:
                keep = jnp.where(chunk == c, pattern_ref[0, 4 * tile + c].astype(F32), keep)
        tiles.append(values * keep)
    rolled = Rolled(tiles)
    for leaf in range(8):
        parts = []
        for q, (w, u) in enumerate(PAIRS):
            block = OFFSET[w, u] + leaf % 2**w
            parts.append(rolled.take(block // 4, block % 4, q % 4))
        out_ref[leaf, :, 0:128] = merge(parts[:4], chunk).astype(BF)
        out_ref[leaf, :, 128:256] = merge(parts[4:], chunk).astype(BF)


def message_kernel(leaf_ref, columns_ref, rhs_ref, out_ref):
    leaf = leaf_ref[0]
    chunk = lane_chunk(32)
    common = []
    sources = []
    for w, u in PAIRS:
        q = PAIRS.index((w, u))
        for i in range(2**w):
            sources.append((leaf // 2**w * 2**w + i, q))
    for tile in range(C_TILES):
        parts = []
        for c in range(4):
            if 4 * tile + c < BLOCKS:
                source, q = sources[4 * tile + c]
                values = columns_ref[source, :, 128 * (q // 4) : 128 * (q // 4) + 128].astype(F32)
                shift = (c - q) % 4 * 32
                parts.append(values if shift == 0 else pltpu.roll(values, shift, 1))
        common.append(merge(parts, chunk).astype(BF))
    rhs = jnp.transpose(rhs_ref[...].reshape(128, 128))
    high = rhs.astype(BF).astype(F32)
    low = rhs - high
    for tile in range(16):
        both = jnp.concatenate([high[8 * tile : 8 * tile + 8], low[8 * tile : 8 * tile + 8]], 0)
        out_ref[tile, 0:RHS_ROWS] = both.astype(BF)
        for n, values in enumerate(common):
            out_ref[tile, C_AT + 32 * n : C_AT + 32 * n + 32] = values


def couple(parts, bd_ref):
    out = []
    for j in range(4):
        total = None
        for vector, m in parts:
            term = dot_nt(vector[:, 128 * j : 128 * j + 128], bd_ref[m, j])
            total = term if total is None else total + term
        out.append(-total)
    return jnp.concatenate(out, 1)


def put_in_order(place_ref, pieces, refs):
    z, x = place_ref[0] // 4, place_ref[0] % 4
    for half in range(2):
        for n in range(4):
            for m in range(4):
                dz, dx = (n, m) if half == 0 else (m, n)
                tile = (z - dz + 4) % 4 * 4 + (x - dx + 4) % 4
                at = pl.multiple_of(tile * 32 + 16 * half, 16)
                first = 0
                for ref in refs:
                    last = first + ref.shape[1]
                    rows = pieces[4 * half + n][16 * m : 16 * m + 16, first:last]
                    ref[pl.ds(at, 16), :] = rows
                    first = last


def stack_kernel(*refs):
    parts, outs = refs[:4], refs[4:]
    first = 0
    for out in outs:
        last = first + out.shape[1]
        for n, part in enumerate(parts):
            out[16 * n : 16 * n + 16, :] = part[:, first:last]
        first = last


def first_kernel(leaf_ref, place_ref, msg_ref, *rest):
    pieces, outs = rest[:8], rest[8:]
    b_ref, bd_ref, d0_ref, d1_ref, d2_ref, y0_ref, p1_ref = outs
    leaf = leaf_ref[0]
    chunk8 = lane_chunk(8)
    rhs = Rolled(
        [msg_ref[t, 0:8].astype(F32) + msg_ref[t, 8:16].astype(F32) for t in range(16)]
    )
    for v in range(4):
        for j in range(4):
            parts = [rhs.take(4 * j + c, v, c) for c in range(4)]
            b_ref[v, :, 128 * j : 128 * j + 128] = merge(parts, chunk8)
    row_chunk = lax.broadcasted_iota(jnp.int32, (128, 128), 0) // 32
    same = row_chunk == lane_chunk(128)
    rows = lax.broadcasted_iota(jnp.int32, (128, 128), 0)
    lanes = lax.broadcasted_iota(jnp.int32, (128, 128), 1)
    pick = [
        jnp.where(rows == lanes % 32 + 32 * c, 1.0, 0.0).astype(BF) for c in range(4)
    ]
    for m in range(BLOCKS):
        at = C_AT + 32 * (m // 4)
        for j in range(4):
            block = msg_ref[4 * j : 4 * j + 4, at : at + 32, :].reshape(128, 128)
            spread = dot_nn(block, pick[m % 4])
            bd_ref[m, j] = jnp.where(same, spread, 0.0).astype(BF)
    put_in_order(place_ref, pieces, (d0_ref, d1_ref, d2_ref))
    y0 = dot_nt(b_ref[0].astype(BF), d0_ref[...]).astype(BF)
    y0_ref[...] = y0
    for i in range(2):
        mine = jnp.where(leaf % 2 == i, b_ref[1], 0.0)
        p1_ref[:, 512 * i : 512 * i + 512] = (couple([(y0, i)], bd_ref) + mine).astype(BF)


def times_rows(z, d_ref, width):
    total = jnp.zeros((8, 512), F32)
    for at in range(0, width, 1024):
        total = total + dot_nt(z[:, at : at + 1024], d_ref[:, at : at + 1024])
    return total


def forward_kernel(level, leaf_ref, own_ref, other_ref, d_ref, b_ref, bd_ref, *rest):
    ys, (y_ref, p_ref) = rest[:-2], rest[-2:]
    leaf = leaf_ref[0]
    z = (own_ref[...].astype(F32) + other_ref[...].astype(F32)).astype(BF)
    y = times_rows(z, d_ref, z.shape[1]).astype(BF)
    y_ref[...] = y
    vectors = [r[...] for r in ys] + [y]
    span = 2 ** (level + 1)
    for i in range(span):
        mine = jnp.where(leaf % span == i, b_ref[level + 1], 0.0)
        parts = [(vec, OFFSET[level + 1, u] + i) for u, vec in enumerate(vectors)]
        p_ref[:, 512 * i : 512 * i + 512] = (couple(parts, bd_ref) + mine).astype(BF)


def top_kernel(own_ref, other_ref, *rest):
    pieces, x_ref = rest[:-1], rest[-1]

    def rows(at):
        return jnp.concatenate([p[:, at : at + 512] for p in pieces], 0)

    z = (own_ref[...].astype(F32) + other_ref[...].astype(F32)).astype(BF)
    y = jnp.zeros((8, 512), F32)
    for at in range(0, 4096, 512):
        y = y + dot_nt(z[:, at : at + 512], rows(at))
    y = y.astype(BF)
    for at in range(0, 4096, 512):
        x_ref[:, at : at + 512] = dot_nn(y, rows(at)).astype(BF)


def back_kernel(level, leaf_ref, own_ref, other_ref, d_ref, y_ref, bd_ref, *rest):
    first = level == 2
    pending = () if first else rest[: level + 1]
    outs = rest[len(pending) :]
    x_ref, xp_ref, next_refs = outs[0], outs[1], outs[2:]
    leaf = leaf_ref[0]
    span = 2 ** (level + 1)
    total = own_ref[...].astype(F32) + other_ref[...].astype(F32)
    x = total.astype(BF)
    mine = total[:, 0:512]
    for i in range(1, span):
        mine = jnp.where(leaf % span == i, total[:, 512 * i : 512 * i + 512], mine)
    x_ref[...] = mine
    for u in range(level + 1):
        columns = []
        for j in range(4):
            term = None
            for i in range(span):
                at = 512 * i + 128 * j
                part = dot_nn(x[:, at : at + 128], bd_ref[OFFSET[level + 1, u] + i, j])
                term = part if term is None else term + part
            columns.append(term)
        p = jnp.concatenate(columns, 1)
        if not first:
            p = p + pending[u][...]
        if u < level:
            next_refs[u][...] = p
        else:
            q = (y_ref[...].astype(F32) - p).astype(BF)
    if level > 0:
        width = 512 * 2**level
        for at in range(0, width, 1024):
            xp_ref[:, at : at + 1024] = dot_nn(q, d_ref[:, at : at + 1024]).astype(BF)
    else:
        xp_ref[...] = dot_nn(q, d_ref[...])


def pack_kernel(x0_ref, x1_ref, x2_ref, x3_ref, out_ref):
    chunk = lane_chunk(8)
    tiles = [r[:, 128 * j : 128 * j + 128] for r in (x0_ref, x1_ref, x2_ref, x3_ref) for j in range(4)]
    rolled = Rolled(tiles)
    for t in range(16):
        parts = [rolled.take(4 * v + t // 4, t % 4, v) for v in range(4)]
        out_ref[t] = merge(parts, chunk)


def shape(dims, kind=BF):
    return jax.ShapeDtypeStruct(dims, kind)


def reduce_over(part, level):
    hops = [
        [(i, i ^ 1) for i in range(8)],
        [(i, i ^ 2) for i in range(8)],
        [(i, (3 - i // 2) * 2 + i % 2) for i in range(8)],
    ]
    for n in range(level):
        other = lax.ppermute(part, "leaf", hops[n])
        if n == level - 1:
            return part, other
        part = (part.astype(F32) + other.astype(F32)).astype(BF)


def shift_x(values, by):
    return lax.ppermute(values, "tile", [(t, t // 4 * 4 + (t + by) % 4) for t in range(16)])


def shift_z(values, by):
    return lax.ppermute(values, "tile", [(t, (t + 4 * by) % 16) for t in range(16)])


def local(right_sides, diag_inverse, coupling, pattern):
    leaf = lax.axis_index("leaf").astype(jnp.int32).reshape(1)
    place = lax.axis_index("tile").astype(jnp.int32).reshape(1)
    upper, lower = diag_inverse[0:16], diag_inverse[16:32]
    upper = [upper] + [shift_x(upper, k) for k in (1, 2, 3)]
    lower = [lower] + [shift_z(lower, k) for k in (1, 2, 3)]

    stack = pl.pallas_call(
        stack_kernel,
        out_shape=(shape((64, 3584)), shape((64, 4096))),
        in_specs=[VMEM] * 4,
        out_specs=(VMEM,) * 2,
        compiler_params=params(),
        name="stack",
    )
    upper1, upper = stack(*upper)
    lower1, lower = stack(*lower)

    def far(upper, lower):
        pieces = [upper] + [shift_z(upper, k) for k in (1, 2, 3)]
        return pieces + [lower] + [shift_x(lower, k) for k in (1, 2, 3)]

    pieces1 = far(upper1, lower1)
    split = pl.pallas_call(
        split_kernel,
        out_shape=shape((8, 32, 256)),
        in_specs=[VMEM, SMEM],
        out_specs=VMEM,
        compiler_params=params(),
        name="split_couplings",
    )(coupling, pattern)
    columns = lax.all_to_all(split, "leaf", 0, 0, tiled=True)
    message_call = pl.pallas_call(
        message_kernel,
        out_shape=shape((16, MESSAGE, 128)),
        in_specs=[SMEM, VMEM, VMEM],
        out_specs=VMEM,
        compiler_params=params(),
        name="message",
    )
    message = message_call(leaf, columns, right_sides)
    message = lax.all_to_all(message, "tile", 0, 0, tiled=True)
    upper, lower, message = lax.optimization_barrier((upper, lower, message))
    pieces3 = far(upper, lower)
    first_call = pl.pallas_call(
        first_kernel,
        out_shape=(
            shape((4, 8, 512), F32),
            shape((BLOCKS, 4, 128, 128)),
            shape((512, 512)),
            shape((512, 1024)),
            shape((512, 2048)),
            shape((8, 512)),
            shape((8, 1024)),
        ),
        in_specs=[SMEM, SMEM] + [VMEM] * 9,
        out_specs=(VMEM,) * 7,
        compiler_params=params(),
        name="level0",
    )
    b, bd, d0, d1, d2, y0, p1 = first_call(leaf, place, message, *pieces1)

    def forward(level, part, d, ys):
        own, other = reduce_over(part, level)
        return pl.pallas_call(
            functools.partial(forward_kernel, level),
            out_shape=(shape((8, 512)), shape((8, 512 * 2 ** (level + 1)))),
            in_specs=[SMEM] + [VMEM] * (5 + len(ys)),
            out_specs=(VMEM,) * 2,
            compiler_params=params(),
        )(leaf, own, other, d, b, bd, *ys)

    y1, p2 = forward(1, p1, d1, (y0,))
    y2, p3 = forward(2, p2, d2, (y0, y1))
    own, other = reduce_over(p3, 3)
    xp = pl.pallas_call(
        top_kernel,
        out_shape=shape((8, 4096)),
        in_specs=[VMEM] * 10,
        out_specs=VMEM,
        compiler_params=params(),
        name="level3",
    )(own, other, *pieces3)

    def back(level, part, d, y, pending):
        own, other = reduce_over(part, level + 1)
        out = [shape((8, 512), F32)]
        out.append(shape((8, 512 * 2**level), BF if level else F32))
        out += [shape((8, 512), F32)] * level
        return pl.pallas_call(
            functools.partial(back_kernel, level),
            out_shape=tuple(out),
            in_specs=[SMEM] + [VMEM] * (5 + len(pending)),
            out_specs=(VMEM,) * len(out),
            compiler_params=params(),
        )(leaf, own, other, d, y, bd, *pending)

    x3, xp, *pending = back(2, xp, d2, y2, ())
    x2, xp, *pending = back(1, xp, d1, y1, pending)
    x1, x0 = back(0, xp, d0, y0, pending)
    packed = pl.pallas_call(
        pack_kernel,
        out_shape=shape((16, 8, 128), F32),
        in_specs=[VMEM] * 4,
        out_specs=VMEM,
        compiler_params=params(),
        name="pack",
    )(x0, x1, x2, x3)
    packed = lax.all_to_all(packed, "tile", 0, 0, tiled=True)
    return jnp.transpose(packed.reshape(128, 128)).reshape(4, 32, 128)


def solution(mesh):
    placed = (
        P(None, ("leaf", "tile"), None),
        P(("leaf", "tile"), None),
        P(("leaf", "tile"), None),
        P(("leaf", "tile"), None),
    )
    return jax.shard_map(
        local,
        mesh=mesh,
        in_specs=placed,
        out_specs=P(None, ("leaf", "tile"), None),
        check_vma=False,
    )
```

```python
import functools

import jax
import jax.numpy as jnp
from jax import lax
from jax.experimental import pallas as pl
from jax.experimental.pallas import tpu as pltpu
from jax.sharding import PartitionSpec as P


BF = jnp.bfloat16
F32 = jnp.float32
PAIRS = ((1, 0), (2, 0), (2, 1), (3, 0), (3, 1), (3, 2))
OFFSET = {(1, 0): 0, (2, 0): 2, (2, 1): 6, (3, 0): 10, (3, 1): 18, (3, 2): 26}
BLOCKS = 34
VMEM = pl.BlockSpec(memory_space=pltpu.VMEM)
SMEM = pl.BlockSpec(memory_space=pltpu.SMEM)
RHS_ROWS, C_TILES = 16, 9
C_AT = RHS_ROWS
MESSAGE = C_AT + 32 * C_TILES


def params(mib=20):
    return pltpu.CompilerParams(vmem_limit_bytes=mib * 2**20)


def lane_chunk(rows):
    return lax.broadcasted_iota(jnp.int32, (rows, 128), 1) // 32


def dot_nt(a, b):
    return lax.dot_general(a, b, (((1,), (1,)), ((), ())), preferred_element_type=F32)


def dot_nn(a, b):
    return jnp.dot(a, b, preferred_element_type=F32)


class Rolled:
    def __init__(self, tiles):
        self.tiles = tiles
        self.made = {}

    def take(self, tile, source, target):
        shift = (target - source) % 4 * 32
        if shift == 0:
            return self.tiles[tile]
        if (tile, shift) not in self.made:
            self.made[tile, shift] = pltpu.roll(self.tiles[tile], shift, 1)
        return self.made[tile, shift]


def merge(parts, chunk):
    result = parts[0]
    for c in range(1, len(parts)):
        result = jnp.where(chunk == c, parts[c], result)
    return result


def split_kernel(coupling_ref, pattern_ref, out_ref):
    chunk = lane_chunk(32)
    tiles = []
    for tile in range(C_TILES):
        if tile < 8:
            values = coupling_ref[:, 128 * tile : 128 * tile + 128].astype(F32)
        else:
            half = coupling_ref[:, 1024:1088].astype(F32)
            values = jnp.concatenate([half, jnp.zeros_like(half)], 1)
        keep = jnp.zeros((32, 128), F32)
        for c in range(4):
            if 4 * tile + c < BLOCKS:
                keep = jnp.where(chunk == c, pattern_ref[0, 4 * tile + c].astype(F32), keep)
        tiles.append(values * keep)
    rolled = Rolled(tiles)
    for leaf in range(8):
        parts = []
        for q, (w, u) in enumerate(PAIRS):
            block = OFFSET[w, u] + leaf % 2**w
            parts.append(rolled.take(block // 4, block % 4, q % 4))
        out_ref[leaf, :, 0:128] = merge(parts[:4], chunk).astype(BF)
        out_ref[leaf, :, 128:256] = merge(parts[4:], chunk).astype(BF)


def message_kernel(leaf_ref, columns_ref, rhs_ref, out_ref):
    leaf = leaf_ref[0]
    chunk = lane_chunk(32)
    common = []
    sources = []
    for w, u in PAIRS:
        q = PAIRS.index((w, u))
        for i in range(2**w):
            sources.append((leaf // 2**w * 2**w + i, q))
    for tile in range(C_TILES):
        parts = []
        for c in range(4):
            if 4 * tile + c < BLOCKS:
                source, q = sources[4 * tile + c]
                values = columns_ref[source, :, 128 * (q // 4) : 128 * (q // 4) + 128].astype(F32)
                shift = (c - q) % 4 * 32
                parts.append(values if shift == 0 else pltpu.roll(values, shift, 1))
        common.append(merge(parts, chunk).astype(BF))
    rhs = jnp.transpose(rhs_ref[...].reshape(128, 128))
    high = rhs.astype(BF).astype(F32)
    low = rhs - high
    for tile in range(16):
        both = jnp.concatenate([high[8 * tile : 8 * tile + 8], low[8 * tile : 8 * tile + 8]], 0)
        out_ref[tile, 0:RHS_ROWS] = both.astype(BF)
        for n, values in enumerate(common):
            out_ref[tile, C_AT + 32 * n : C_AT + 32 * n + 32] = values


def couple(parts, bd_ref):
    out = []
    for j in range(4):
        total = None
        for vector, m in parts:
            term = dot_nt(vector[:, 128 * j : 128 * j + 128], bd_ref[m, j])
            total = term if total is None else total + term
        out.append(-total)
    return jnp.concatenate(out, 1)


def put_in_order(place_ref, pieces, refs):
    z, x = place_ref[0] // 4, place_ref[0] % 4
    for half in range(2):
        for n in range(4):
            for m in range(4):
                dz, dx = (n, m) if half == 0 else (m, n)
                tile = (z - dz + 4) % 4 * 4 + (x - dx + 4) % 4
                at = pl.multiple_of(tile * 32 + 16 * half, 16)
                first = 0
                for ref in refs:
                    last = first + ref.shape[1]
                    rows = pieces[4 * half + n][16 * m : 16 * m + 16, first:last]
                    ref[pl.ds(at, 16), :] = rows
                    first = last


def order_kernel(place_ref, *rest):
    put_in_order(place_ref, rest[:-1], rest[-1:])


def stack_kernel(*refs):
    parts, outs = refs[:4], refs[4:]
    first = 0
    for out in outs:
        last = first + out.shape[1]
        for n, part in enumerate(parts):
            out[16 * n : 16 * n + 16, :] = part[:, first:last]
        first = last


def first_kernel(leaf_ref, place_ref, msg_ref, *rest):
    pieces, outs = rest[:8], rest[8:]
    b_ref, bd_ref, d0_ref, d1_ref, y0_ref, p1_ref = outs
    leaf = leaf_ref[0]
    chunk8 = lane_chunk(8)
    rhs = Rolled(
        [msg_ref[t, 0:8].astype(F32) + msg_ref[t, 8:16].astype(F32) for t in range(16)]
    )
    for v in range(4):
        for j in range(4):
            parts = [rhs.take(4 * j + c, v, c) for c in range(4)]
            b_ref[v, :, 128 * j : 128 * j + 128] = merge(parts, chunk8)
    row_chunk = lax.broadcasted_iota(jnp.int32, (128, 128), 0) // 32
    same = row_chunk == lane_chunk(128)
    rows = lax.broadcasted_iota(jnp.int32, (128, 128), 0)
    lanes = lax.broadcasted_iota(jnp.int32, (128, 128), 1)
    pick = [
        jnp.where(rows == lanes % 32 + 32 * c, 1.0, 0.0).astype(BF) for c in range(4)
    ]
    for m in range(BLOCKS):
        at = C_AT + 32 * (m // 4)
        for j in range(4):
            block = msg_ref[4 * j : 4 * j + 4, at : at + 32, :].reshape(128, 128)
            spread = dot_nn(block, pick[m % 4])
            bd_ref[m, j] = jnp.where(same, spread, 0.0).astype(BF)
    put_in_order(place_ref, pieces, (d0_ref, d1_ref))
    y0 = dot_nt(b_ref[0].astype(BF), d0_ref[...]).astype(BF)
    y0_ref[...] = y0
    for i in range(2):
        mine = jnp.where(leaf % 2 == i, b_ref[1], 0.0)
        p1_ref[:, 512 * i : 512 * i + 512] = (couple([(y0, i)], bd_ref) + mine).astype(BF)


def times_rows(z, d_ref, width):
    total = jnp.zeros((8, 512), F32)
    for at in range(0, width, 1024):
        total = total + dot_nt(z[:, at : at + 1024], d_ref[:, at : at + 1024])
    return total


def forward_kernel(level, leaf_ref, own_ref, other_ref, d_ref, b_ref, bd_ref, *rest):
    ys, (y_ref, p_ref) = rest[:-2], rest[-2:]
    leaf = leaf_ref[0]
    z = (own_ref[...].astype(F32) + other_ref[...].astype(F32)).astype(BF)
    y = times_rows(z, d_ref, z.shape[1]).astype(BF)
    y_ref[...] = y
    vectors = [r[...] for r in ys] + [y]
    span = 2 ** (level + 1)
    for i in range(span):
        mine = jnp.where(leaf % span == i, b_ref[level + 1], 0.0)
        parts = [(vec, OFFSET[level + 1, u] + i) for u, vec in enumerate(vectors)]
        p_ref[:, 512 * i : 512 * i + 512] = (couple(parts, bd_ref) + mine).astype(BF)


def top_kernel(own_ref, other_ref, *rest):
    pieces, x_ref = rest[:-1], rest[-1]

    def rows(at):
        return jnp.concatenate([p[:, at : at + 512] for p in pieces], 0)

    z = (own_ref[...].astype(F32) + other_ref[...].astype(F32)).astype(BF)
    y = jnp.zeros((8, 512), F32)
    for at in range(0, 4096, 512):
        y = y + dot_nt(z[:, at : at + 512], rows(at))
    y = y.astype(BF)
    for at in range(0, 4096, 512):
        x_ref[:, at : at + 512] = dot_nn(y, rows(at)).astype(BF)


def back_kernel(level, leaf_ref, own_ref, other_ref, d_ref, y_ref, bd_ref, *rest):
    first = level == 2
    pending = () if first else rest[: level + 1]
    outs = rest[len(pending) :]
    x_ref, xp_ref, next_refs = outs[0], outs[1], outs[2:]
    leaf = leaf_ref[0]
    span = 2 ** (level + 1)
    total = own_ref[...].astype(F32) + other_ref[...].astype(F32)
    x = total.astype(BF)
    mine = total[:, 0:512]
    for i in range(1, span):
        mine = jnp.where(leaf % span == i, total[:, 512 * i : 512 * i + 512], mine)
    x_ref[...] = mine
    for u in range(level + 1):
        columns = []
        for j in range(4):
            term = None
            for i in range(span):
                at = 512 * i + 128 * j
                part = dot_nn(x[:, at : at + 128], bd_ref[OFFSET[level + 1, u] + i, j])
                term = part if term is None else term + part
            columns.append(term)
        p = jnp.concatenate(columns, 1)
        if not first:
            p = p + pending[u][...]
        if u < level:
            next_refs[u][...] = p
        else:
            q = (y_ref[...].astype(F32) - p).astype(BF)
    if level > 0:
        width = 512 * 2**level
        for at in range(0, width, 1024):
            xp_ref[:, at : at + 1024] = dot_nn(q, d_ref[:, at : at + 1024]).astype(BF)
    else:
        xp_ref[...] = dot_nn(q, d_ref[...])


def pack_kernel(x0_ref, x1_ref, x2_ref, x3_ref, out_ref):
    chunk = lane_chunk(8)
    tiles = [r[:, 128 * j : 128 * j + 128] for r in (x0_ref, x1_ref, x2_ref, x3_ref) for j in range(4)]
    rolled = Rolled(tiles)
    for t in range(16):
        parts = [rolled.take(4 * v + t // 4, t % 4, v) for v in range(4)]
        out_ref[t] = merge(parts, chunk).astype(BF)


def shape(dims, kind=BF):
    return jax.ShapeDtypeStruct(dims, kind)


def reduce_over(part, level):
    hops = [
        [(i, i ^ 1) for i in range(8)],
        [(i, i ^ 2) for i in range(8)],
        [(i, (3 - i // 2) * 2 + i % 2) for i in range(8)],
    ]
    for n in range(level):
        other = lax.ppermute(part, "leaf", hops[n])
        if n == level - 1:
            return part, other
        part = (part.astype(F32) + other.astype(F32)).astype(BF)


def shift_x(values, by):
    return lax.ppermute(values, "tile", [(t, t // 4 * 4 + (t + by) % 4) for t in range(16)])


def shift_z(values, by):
    return lax.ppermute(values, "tile", [(t, (t + 4 * by) % 16) for t in range(16)])


def local(right_sides, diag_inverse, coupling, pattern):
    leaf = lax.axis_index("leaf").astype(jnp.int32).reshape(1)
    place = lax.axis_index("tile").astype(jnp.int32).reshape(1)
    upper, lower = diag_inverse[0:16], diag_inverse[16:32]
    upper = [upper] + [shift_x(upper, k) for k in (1, 2, 3)]
    lower = [lower] + [shift_z(lower, k) for k in (1, 2, 3)]

    stack = pl.pallas_call(
        stack_kernel,
        out_shape=(shape((64, 1536)), shape((64, 2048)), shape((64, 4096))),
        in_specs=[VMEM] * 4,
        out_specs=(VMEM,) * 3,
        compiler_params=params(),
        name="stack",
    )
    upper1, upper2, upper = stack(*upper)
    lower1, lower2, lower = stack(*lower)

    def far(upper, lower):
        pieces = [upper] + [shift_z(upper, k) for k in (1, 2, 3)]
        return pieces + [lower] + [shift_x(lower, k) for k in (1, 2, 3)]

    pieces1 = far(upper1, lower1)
    pieces2 = far(upper2, lower2)
    split = pl.pallas_call(
        split_kernel,
        out_shape=shape((8, 32, 256)),
        in_specs=[VMEM, SMEM],
        out_specs=VMEM,
        compiler_params=params(),
        name="split_couplings",
    )(coupling, pattern)
    columns = lax.all_to_all(split, "leaf", 0, 0, tiled=True)
    message_call = pl.pallas_call(
        message_kernel,
        out_shape=shape((16, MESSAGE, 128)),
        in_specs=[SMEM, VMEM, VMEM],
        out_specs=VMEM,
        compiler_params=params(),
        name="message",
    )
    message = message_call(leaf, columns, right_sides)
    message = lax.all_to_all(message, "tile", 0, 0, tiled=True)
    upper, lower, message = lax.optimization_barrier((upper, lower, message))
    pieces3 = far(upper, lower)
    first_call = pl.pallas_call(
        first_kernel,
        out_shape=(
            shape((4, 8, 512), F32),
            shape((BLOCKS, 4, 128, 128)),
            shape((512, 512)),
            shape((512, 1024)),
            shape((8, 512)),
            shape((8, 1024)),
        ),
        in_specs=[SMEM, SMEM] + [VMEM] * 9,
        out_specs=(VMEM,) * 6,
        compiler_params=params(),
        name="level0",
    )
    b, bd, d0, d1, y0, p1 = first_call(leaf, place, message, *pieces1)

    order_call = pl.pallas_call(
        order_kernel,
        out_shape=shape((512, 2048)),
        in_specs=[SMEM] + [VMEM] * 8,
        out_specs=VMEM,
        compiler_params=params(),
        name="order2",
    )
    d2 = order_call(place, *pieces2)

    def forward(level, part, d, ys):
        own, other = reduce_over(part, level)
        return pl.pallas_call(
            functools.partial(forward_kernel, level),
            out_shape=(shape((8, 512)), shape((8, 512 * 2 ** (level + 1)))),
            in_specs=[SMEM] + [VMEM] * (5 + len(ys)),
            out_specs=(VMEM,) * 2,
            compiler_params=params(),
        )(leaf, own, other, d, b, bd, *ys)

    y1, p2 = forward(1, p1, d1, (y0,))
    y2, p3 = forward(2, p2, d2, (y0, y1))
    own, other = reduce_over(p3, 3)
    xp = pl.pallas_call(
        top_kernel,
        out_shape=shape((8, 4096)),
        in_specs=[VMEM] * 10,
        out_specs=VMEM,
        compiler_params=params(),
        name="level3",
    )(own, other, *pieces3)

    def back(level, part, d, y, pending):
        own, other = reduce_over(part, level + 1)
        out = [shape((8, 512), F32)]
        out.append(shape((8, 512 * 2**level), BF if level else F32))
        out += [shape((8, 512), F32)] * level
        return pl.pallas_call(
            functools.partial(back_kernel, level),
            out_shape=tuple(out),
            in_specs=[SMEM] + [VMEM] * (5 + len(pending)),
            out_specs=(VMEM,) * len(out),
            compiler_params=params(),
        )(leaf, own, other, d, y, bd, *pending)

    x3, xp, *pending = back(2, xp, d2, y2, ())
    x2, xp, *pending = back(1, xp, d1, y1, pending)
    x1, x0 = back(0, xp, d0, y0, pending)
    packed = pl.pallas_call(
        pack_kernel,
        out_shape=shape((16, 8, 128)),
        in_specs=[VMEM] * 4,
        out_specs=VMEM,
        compiler_params=params(),
        name="pack",
    )(x0, x1, x2, x3)
    packed = lax.all_to_all(packed, "tile", 0, 0, tiled=True)
    return jnp.transpose(packed.reshape(128, 128).astype(F32)).reshape(4, 32, 128)


def solution(mesh):
    placed = (
        P(None, ("leaf", "tile"), None),
        P(("leaf", "tile"), None),
        P(("leaf", "tile"), None),
        P(("leaf", "tile"), None),
    )
    return jax.shard_map(
        local,
        mesh=mesh,
        in_specs=placed,
        out_specs=P(None, ("leaf", "tile"), None),
        check_vma=False,
    )
```
